512 devices in a mesh: seq: 32 (over x, z), doc: 16 (over y, core).
Axes of the slice: x: 4, y: 8, z: 8, core: 2. Of those that a mesh axis runs over, the one named last changes fastest.
Arguments:
- queries: bfloat16 [65536, 2048], P(('doc', 'seq')), parts along dimension 0, may hold values from -5 to 5
- key_rows: bfloat16 [65536, 2048], P(('doc', 'seq')), parts along dimension 0, may hold values from -5 to 5
- value_rows: bfloat16 [65536, 2048], P(('doc', 'seq')), parts along dimension 0, may hold values from -6 to 6
- out_grad: bfloat16 [65536, 2048], P(('doc', 'seq')), parts along dimension 0, may hold values from -6 to 6
- vertical: int32 [256, 6], P('doc'), parts along dimension 0, may hold values from 0 to 31, as said below
- slash_offsets: int32 [256, 6], P('doc'), parts along dimension 0, may hold values from -31 to 31, as said below
- counts: int32 [256, 2], P('doc'), parts along dimension 0, may hold values from 1 to 6, as said below
Outputs:
- query_grad: bfloat16 [65536, 2048], P(('doc', 'seq')), parts along dimension 0
- key_grad: bfloat16 [65536, 2048], P(('doc', 'seq')), parts along dimension 0
- value_grad: bfloat16 [65536, 2048], P(('doc', 'seq')), parts along dimension 0
The draws below stay inside these ranges and needn't reach their ends.
There are 16 independent parts, one for each index of `doc`. The reference program is written for one: setup_inputs(seed, part) draws one part's arguments, and reference() takes and returns one part's arrays. A program takes and returns all parts, laid end to end along the dimension named above; each array names one. Nothing has to cross between parts.
Inputs may be any that keep to these rules, and one draw needn't show every extreme that they name: counts[h, 0] is 1 to 6 and counts[h, 1] is 1 to 6; some head has both at their most and some head both at 1. `vertical`: the entries of a head are distinct. `slash_offsets`: the entries of a head are distinct and slash_offsets[h, 0] is 0 for every head.
All inputs are finite; a program needn't handle non-finite values.
Results may differ from the reference program's by a relative error of at most 0.0086.
Values may be sent and summed in bfloat16 or wider, within the bound.
No kernel may reach another device: no remote copies, remote signals or barrier semaphores. Data moves between devices by JAX's collectives and lax.ppermute only.
A program may use at most 64 MiB of HBM per device.

```python
import jax
import jax.numpy as jnp
from jax import lax

HEADS = 16
HEAD_DIM = 128
BLK = 128
NV = 6
NS = 6
SEQ_LEN = 4096
BLOCKS = 32


def draw_queries(key, part):
    base = jnp.clip(jax.random.normal(jax.random.fold_in(key, 1), (SEQ_LEN, HEADS * HEAD_DIM)), -4.0, 4.0)
    return base.astype(jnp.bfloat16)


def draw_key_rows(key, part):
    base = jnp.clip(jax.random.normal(jax.random.fold_in(key, 4), (SEQ_LEN, HEADS * HEAD_DIM)), -4.0, 4.0)
    return base.astype(jnp.bfloat16)


def draw_counts(key, part):

    def skewed(base_key, most):
        first_pick = jax.random.randint(jax.random.fold_in(base_key, 0), (HEADS,), 1, most + 1)
        second_pick = jax.random.randint(jax.random.fold_in(base_key, 1), (HEADS,), 1, most + 1)
        return jnp.minimum(first_pick, second_pick)
    vert_count = skewed(jax.random.fold_in(key, 21), NV)
    slash_count = skewed(jax.random.fold_in(key, 22), NS)
    order = jax.random.permutation(jax.random.fold_in(key, 23), HEADS)
    head_ids = jnp.arange(HEADS)
    vert_count = jnp.where(head_ids == order[0], NV, jnp.where(head_ids == order[1], 1, vert_count))
    slash_count = jnp.where(head_ids == order[0], NS, jnp.where(head_ids == order[1], 1, slash_count))
    return jnp.stack([vert_count, slash_count], axis=1).astype(jnp.int32)


def draw_vertical(key, part):
    head_keys = jax.random.split(jax.random.fold_in(key, 31), HEADS)
    picked = jax.vmap(lambda head_key: jax.random.permutation(head_key, BLOCKS)[:NV])(head_keys)
    return picked.astype(jnp.int32)


def draw_slash_offsets(key, part):
    head_keys = jax.random.split(jax.random.fold_in(key, 41), HEADS)
    sizes_drawn = jax.vmap(lambda head_key: jax.random.permutation(head_key, BLOCKS - 1)[:NS - 1] + 1)(head_keys)
    signs = jax.random.randint(jax.random.fold_in(key, 42), (HEADS, NS - 1), 0, 2) * 2 - 1
    offsets = jnp.concatenate([jnp.zeros((HEADS, 1), jnp.int32), (sizes_drawn * signs).astype(jnp.int32)], axis=1)
    return offsets.astype(jnp.int32)


def block_levels(own_key, shape, pieces, smallest, top_value):
    def one(dim, shards_of):
        draws = jax.random.uniform(jax.random.fold_in(jax.random.fold_in(own_key, 6), dim), (shards_of,), jnp.float32, smallest / len(pieces), top_value / len(pieces))
        return jnp.repeat(jnp.exp(draws), shape[dim] // shards_of).reshape((-1,) + (1,) * (len(shape) - dim - 1))

    factor_of = one(*pieces[0])
    for cut in pieces[1:]:
        factor_of = factor_of * one(*cut)
    return factor_of


def normal_values(rng, shape, deviation, bound, cuts=(), held_as=jnp.bfloat16):
    level = block_levels(rng, shape, cuts, -0.22, 0.18) if cuts else 1.0
    values = jax.random.normal(rng, shape, jnp.float32) * deviation * level
    return jnp.minimum(jnp.maximum(values, -bound), bound).astype(held_as)


def setup_inputs(seed: int = 0, part: int = 0) -> dict:
    key_of = jax.random.split(jax.random.key(seed), 8)
    part_splits = jax.random.split(jax.random.fold_in(key_of[7], part), 8)
    queries = draw_queries(jax.random.fold_in(jax.random.fold_in(key_of[7], part), 71), part)
    key_rows = draw_key_rows(jax.random.fold_in(jax.random.fold_in(key_of[7], part), 71), part)
    value_rows = normal_values(part_splits[2], (SEQ_LEN, HEADS * HEAD_DIM), 1.0, 6.0, ((0, 32),))
    out_grad = normal_values(part_splits[3], (SEQ_LEN, HEADS * HEAD_DIM), 1.0, 6.0, ((0, 32),))
    vertical = draw_vertical(jax.random.fold_in(jax.random.fold_in(key_of[7], part), 71), part)
    slash_offsets = draw_slash_offsets(jax.random.fold_in(jax.random.fold_in(key_of[7], part), 71), part)
    counts = draw_counts(jax.random.fold_in(jax.random.fold_in(key_of[7], part), 71), part)
    return dict(queries=queries, key_rows=key_rows, value_rows=value_rows, out_grad=out_grad, vertical=vertical, slash_offsets=slash_offsets, counts=counts)


block_group = 4


def block_lists(chosen, vert_head, slash_head, count_head, nblocks):
    vert_cap = vert_head.shape[0]
    slash_cap = slash_head.shape[0]
    rows_now = chosen.shape[0]
    vert_index = jnp.broadcast_to(vert_head[None, :], (rows_now, vert_cap))
    vert_valid = jnp.broadcast_to((jnp.arange(vert_cap, dtype=jnp.int32) < count_head[0])[None, :], (rows_now, vert_cap))
    slash_index = chosen[:, None] - slash_head[None, :]
    inside = (slash_index >= 0) & (slash_index < nblocks)
    repeated = jnp.any((vert_index[:, :, None] == slash_index[:, None, :]) & vert_valid[:, :, None], axis=1)
    slash_valid = (jnp.arange(slash_cap, dtype=jnp.int32) < count_head[1])[None, :] & inside & jnp.logical_not(repeated)
    index_table = jnp.clip(jnp.concatenate([vert_index, slash_index], axis=1), 0, nblocks - 1).astype(jnp.int32)
    valid_table = jnp.concatenate([vert_valid, slash_valid], axis=1)
    return index_table, valid_table


def head_reference(operands):
    q_blocks, k_blocks, v_blocks, d_blocks, vert_head, slash_head, count_head = operands
    nblocks, blk_rows, head_dim = q_blocks.shape
    score_scale = head_dim ** -0.5
    highest = lax.Precision.HIGHEST

    def one_group(carried, chosen):
        key_acc, value_acc = carried
        index_table, valid_table = block_lists(chosen, vert_head, slash_head, count_head, nblocks)
        groups_now, slot_count = index_table.shape
        q_group = q_blocks[chosen].astype(jnp.float32)
        d_group = d_blocks[chosen].astype(jnp.float32)
        k_tiles = k_blocks[index_table].reshape(groups_now, slot_count * blk_rows, head_dim).astype(jnp.float32)
        v_tiles = v_blocks[index_table].reshape(groups_now, slot_count * blk_rows, head_dim).astype(jnp.float32)
        allowed = jnp.repeat(valid_table, blk_rows, axis=1)[:, None, :]
        scores = jnp.einsum("gqd,gkd->gqk", q_group, k_tiles, precision=highest) * score_scale
        scores = jnp.where(allowed, scores, -1e30)
        row_top = jnp.max(scores, axis=-1, keepdims=True)
        expd = jnp.where(allowed, jnp.exp(scores - row_top), 0.0)
        probs = expd / jnp.sum(expd, axis=-1, keepdims=True)
        weights = lax.optimization_barrier(probs.astype(jnp.bfloat16)).astype(jnp.float32)
        attended = jnp.einsum("gqk,gkd->gqd", weights, v_tiles, precision=highest)
        row_delta = jnp.sum(d_group * attended, axis=-1, keepdims=True)
        grad_probs = jnp.einsum("gqd,gkd->gqk", d_group, v_tiles, precision=highest)
        grad_scores = lax.optimization_barrier((probs * (grad_probs - row_delta)).astype(jnp.bfloat16)).astype(jnp.float32)
        query_part = jnp.einsum("gqk,gkd->gqd", grad_scores, k_tiles, precision=highest) * score_scale
        key_part = jnp.einsum("gqk,gqd->gkd", grad_scores, q_group, precision=highest) * score_scale
        value_part = jnp.einsum("gqk,gqd->gkd", weights, d_group, precision=highest)
        flat_index = index_table.reshape(-1)
        key_acc = key_acc.at[flat_index].add(key_part.reshape(groups_now * slot_count, blk_rows, head_dim))
        value_acc = value_acc.at[flat_index].add(value_part.reshape(groups_now * slot_count, blk_rows, head_dim))
        return (key_acc, value_acc), query_part

    zeros_acc = jnp.zeros((nblocks, blk_rows, head_dim), jnp.float32)
    chosen_all = jnp.arange(nblocks, dtype=jnp.int32).reshape(-1, block_group)
    (key_acc, value_acc), query_grad = lax.scan(one_group, (zeros_acc, zeros_acc), chosen_all)
    return query_grad.reshape(nblocks, blk_rows, head_dim), key_acc, value_acc


def reference(queries, key_rows, value_rows, out_grad, vertical, slash_offsets, counts):
    length = queries.shape[0]
    nblocks = length // BLK

    def by_head(matrix):
        return matrix.reshape(nblocks, BLK, HEADS, HEAD_DIM).transpose(2, 0, 1, 3)

    results = lax.map(head_reference, (by_head(queries), by_head(key_rows), by_head(value_rows), by_head(out_grad), vertical, slash_offsets, counts))

    def joined(blocks):
        return blocks.transpose(1, 2, 0, 3).reshape(length, HEADS * HEAD_DIM).astype(jnp.bfloat16)

    return joined(results[0]), joined(results[1]), joined(results[2])
```

```python
import functools

import jax
import jax.numpy as jnp
from jax import lax
from jax.experimental import pallas as pl
from jax.experimental.pallas import tpu as pltpu
from jax.sharding import Mesh
from jax.sharding import PartitionSpec as P

HEADS = 16
HEAD_DIM = 128
BLK = 128
NBLOCKS = 32
HALF = NBLOCKS // 2
SLOTS = 12
SCALE = HEAD_DIM ** (-0.5)
ORDER = ("zl", "x", "zh")
SWAP = [(0, 1), (1, 0)]
NEG = -1e30
VMEM_SPEC = pl.BlockSpec(memory_space=pltpu.VMEM)
SMEM_SPEC = pl.BlockSpec(memory_space=pltpu.SMEM)


def split_kernel(sc_ref, q_ref, k_ref, v_ref, d_ref, keep_ref, send_ref):
    heads_now = q_ref.shape[1] // HEAD_DIM

    def put(ref, first, second):
        for h in range(heads_now):
            cols = slice(h * HEAD_DIM, (h + 1) * HEAD_DIM)
            ref[h, 0] = first[:, cols]
            ref[h, 1] = second[:, cols]

    @pl.when(sc_ref[1] == 1)
    def _():
        put(keep_ref.at[0], q_ref, d_ref)
        put(send_ref, k_ref, v_ref)

    @pl.when(sc_ref[1] == 0)
    def _():
        put(keep_ref.at[0], k_ref, v_ref)
        put(send_ref, q_ref, d_ref)


def split_call(scalars, q, k, v, d):
    step_heads = 4
    in_spec = pl.BlockSpec((BLK, step_heads * HEAD_DIM), lambda g, sc: (0, g))
    return pl.pallas_call(
        split_kernel,
        grid_spec=pltpu.PrefetchScalarGridSpec(
            num_scalar_prefetch=1,
            grid=(HEADS // step_heads,),
            in_specs=[in_spec] * 4,
            out_specs=[
                pl.BlockSpec((1, step_heads, 2, BLK, HEAD_DIM), lambda g, sc: (sc[0], g, 0, 0, 0)),
                pl.BlockSpec((step_heads, 2, BLK, HEAD_DIM), lambda g, sc: (g, 0, 0, 0)),
            ],
        ),
        out_shape=[
            jax.ShapeDtypeStruct((2, HEADS, 2, BLK, HEAD_DIM), jnp.bfloat16),
            jax.ShapeDtypeStruct((HEADS, 2, BLK, HEAD_DIM), jnp.bfloat16),
        ],
        name="split_heads",
    )(scalars, q, k, v, d)


def attend_kernel(
    sc_ref, tab_ref, y_ref, z_ref, dq_ref, send_ref, loc_ref, kv, kt, acc, s_buf, g_buf
):
    core = sc_ref[0]

    def load_keys(t, ref, m, lead):
        k_tile = ref[lead + (m, 0)]
        kv[t, :, :HEAD_DIM] = k_tile
        kv[t, :, HEAD_DIM:] = ref[lead + (m, 1)]
        kt[t] = k_tile.T
        acc[t] = jnp.zeros((BLK, 2 * HEAD_DIM), jnp.float32)

    @pl.loop(0, HALF)
    def _(m):
        load_keys(m, z_ref, m, ())
        load_keys(HALF + m, y_ref, m, (1 - core,))

    zero = jnp.zeros((HEAD_DIM, HEAD_DIM), jnp.bfloat16)

    def diagonal(first, second):
        return jnp.concatenate(
            [jnp.concatenate([first, zero], axis=1), jnp.concatenate([zero, second], axis=1)],
            axis=0,
        )

    @pl.loop(0, HALF)
    def _(m):
        q = y_ref[core, m, 0]
        d = y_ref[core, m, 1]
        into_scores = diagonal(q.T, d.T)
        into_grads = diagonal(q, d)
        count = tab_ref[m, SLOTS]
        pairs = (count + 1) // 2

        def scores_step(g, top):
            for u in range(2):
                a = 2 * g + u
                t = tab_ref[m, a]
                both = jnp.dot(kv[t], into_scores, preferred_element_type=jnp.float32)
                s = both[:, :BLK] + jnp.where(a < count, 0.0, NEG)
                s_buf[a] = s
                g_buf[a] = both[:, BLK:]
                top = jnp.maximum(top, jnp.max(s, axis=0, keepdims=True))
            return top

        top = lax.fori_loop(0, pairs, scores_step, jnp.full((1, BLK), NEG, jnp.float32))

        def exp_step(g, sums):
            total, weighted = sums
            for u in range(2):
                a = 2 * g + u
                e = jnp.exp((s_buf[a] - top) * SCALE)
                s_buf[a] = e
                total = total + jnp.sum(e, axis=0, keepdims=True)
                weighted = weighted + jnp.sum(e * g_buf[a], axis=0, keepdims=True)
            return total, weighted

        zero_row = jnp.zeros((1, BLK), jnp.float32)
        total, weighted = lax.fori_loop(0, pairs, exp_step, (zero_row, zero_row))
        inverse = 1.0 / total
        delta = weighted * inverse

        def grad_step(g, dq_t):
            for u in range(2):
                a = 2 * g + u
                t = tab_ref[m, a]
                p = s_buf[a] * inverse
                w = p.astype(jnp.bfloat16)
                ds = (p * (g_buf[a] - delta)).astype(jnp.bfloat16)
                acc[t] += jnp.dot(
                    jnp.concatenate([ds, w], axis=1), into_grads, preferred_element_type=jnp.float32
                )
                dq_t = dq_t + jnp.dot(kt[t], ds, preferred_element_type=jnp.float32)
            return dq_t

        dq_t = lax.fori_loop(0, pairs, grad_step, jnp.zeros((HEAD_DIM, BLK), jnp.float32))
        dq_ref[m] = (dq_t * SCALE).T.astype(jnp.bfloat16)

    hb = BLK // 2

    @pl.loop(0, HALF)
    def _(m):
        near = acc[m]
        far = acc[HALF + m]
        send_ref[m, :BLK] = (near[:, :HEAD_DIM] * SCALE).astype(jnp.bfloat16)
        send_ref[m, BLK : BLK + hb] = near[hb:, HEAD_DIM:].astype(jnp.bfloat16)
        send_ref[m, BLK + hb :] = far[:hb, HEAD_DIM:].astype(jnp.bfloat16)
        loc_ref[m, :BLK] = far[:, :HEAD_DIM] * SCALE
        loc_ref[m, BLK : BLK + hb] = far[hb:, HEAD_DIM:]
        loc_ref[m, BLK + hb :] = near[:hb, HEAD_DIM:]


def attend_call(scalars, table, y, z):
    return pl.pallas_call(
        attend_kernel,
        in_specs=[SMEM_SPEC, SMEM_SPEC, VMEM_SPEC, VMEM_SPEC],
        out_specs=[VMEM_SPEC, VMEM_SPEC, VMEM_SPEC],
        out_shape=[
            jax.ShapeDtypeStruct((HALF, BLK, HEAD_DIM), jnp.bfloat16),
            jax.ShapeDtypeStruct((HALF, 2 * BLK, HEAD_DIM), jnp.bfloat16),
            jax.ShapeDtypeStruct((HALF, 2 * BLK, HEAD_DIM), jnp.float32),
        ],
        scratch_shapes=[
            pltpu.VMEM((NBLOCKS, BLK, 2 * HEAD_DIM), jnp.bfloat16),
            pltpu.VMEM((NBLOCKS, HEAD_DIM, BLK), jnp.bfloat16),
            pltpu.VMEM((NBLOCKS, BLK, 2 * HEAD_DIM), jnp.float32),
            pltpu.VMEM((SLOTS, BLK, BLK), jnp.float32),
            pltpu.VMEM((SLOTS, BLK, BLK), jnp.float32),
        ],
        compiler_params=pltpu.CompilerParams(vmem_limit_bytes=40 * 1024 * 1024),
        name="attend",
    )(scalars, table, y, z)


def join_kernel(sc_ref, dq_ref, loc_ref, got_ref, out_ref):
    core = sc_ref[0]
    hb = BLK // 2
    summed = (loc_ref[...] + got_ref[...].astype(jnp.float32)).astype(jnp.bfloat16)
    out_ref[core, :, :BLK] = dq_ref[...]
    out_ref[core, :, BLK:] = summed[:, BLK + hb :]
    out_ref[1 - core] = summed[:, : BLK + hb]


def join_call(scalars, dq, loc, got):
    return pl.pallas_call(
        join_kernel,
        in_specs=[SMEM_SPEC, VMEM_SPEC, VMEM_SPEC, VMEM_SPEC],
        out_specs=VMEM_SPEC,
        out_shape=jax.ShapeDtypeStruct((2, HALF, BLK + BLK // 2, HEAD_DIM), jnp.bfloat16),
        compiler_params=pltpu.CompilerParams(vmem_limit_bytes=40 * 1024 * 1024),
        name="join_partials",
    )(scalars, dq, loc, got)


def merge_kernel(sc_ref, own_ref, got_ref, dq_ref, dk_ref, dv_ref):
    heads_now = dq_ref.shape[1] // HEAD_DIM
    hb = BLK // 2

    def put(first, second):
        for h in range(heads_now):
            cols = slice(h * HEAD_DIM, (h + 1) * HEAD_DIM)
            dq_ref[:, cols] = first[h, :BLK]
            dv_ref[:hb, cols] = first[h, BLK:]
            dk_ref[:, cols] = second[h, :BLK]
            dv_ref[hb:, cols] = second[h, BLK:]

    @pl.when(sc_ref[1] == 1)
    def _():
        put(own_ref.at[0], got_ref)

    @pl.when(sc_ref[1] == 0)
    def _():
        put(got_ref, own_ref.at[0])


def merge_call(scalars, own, got):
    step_heads = 4
    out_spec = pl.BlockSpec((BLK, step_heads * HEAD_DIM), lambda g, sc: (0, g))
    rows = BLK + BLK // 2
    return pl.pallas_call(
        merge_kernel,
        grid_spec=pltpu.PrefetchScalarGridSpec(
            num_scalar_prefetch=1,
            grid=(HEADS // step_heads,),
            in_specs=[
                pl.BlockSpec((1, step_heads, rows, HEAD_DIM), lambda g, sc: (sc[0], g, 0, 0)),
                pl.BlockSpec((step_heads, rows, HEAD_DIM), lambda g, sc: (g, 0, 0)),
            ],
            out_specs=[out_spec] * 3,
        ),
        out_shape=[jax.ShapeDtypeStruct((BLK, HEADS * HEAD_DIM), jnp.bfloat16)] * 3,
        name="merge_heads",
    )(scalars, own, got)


def block_table(vert, slash, count, core):
    chosen = core + 2 * jnp.arange(HALF, dtype=jnp.int32)
    vert_index = jnp.broadcast_to(vert[None, :], (HALF, vert.shape[0]))
    vert_valid = jnp.broadcast_to(
        (jnp.arange(vert.shape[0], dtype=jnp.int32) < count[0])[None, :], vert_index.shape
    )
    slash_index = chosen[:, None] - slash[None, :]
    inside = (slash_index >= 0) & (slash_index < NBLOCKS)
    repeated = jnp.any(
        (vert_index[:, :, None] == slash_index[:, None, :]) & vert_valid[:, :, None], axis=1
    )
    slash_valid = (
        (jnp.arange(slash.shape[0], dtype=jnp.int32) < count[1])[None, :]
        & inside
        & jnp.logical_not(repeated)
    )
    index = jnp.concatenate([vert_index, slash_index], axis=1)
    valid = jnp.concatenate([vert_valid, slash_valid], axis=1)
    place = ((index & 1) ^ core) * HALF + (index >> 1)
    rank = jnp.cumsum(valid.astype(jnp.int32), axis=1) - 1
    lanes = jnp.arange(SLOTS, dtype=jnp.int32)
    hit = valid[:, :, None] & (rank[:, :, None] == lanes[None, None, :])
    packed = jnp.sum(jnp.where(hit, place[:, :, None], 0), axis=1)
    total = jnp.sum(valid.astype(jnp.int32), axis=1, keepdims=True)
    return jnp.concatenate([packed, total], axis=1)


def body(queries, key_rows, value_rows, out_grad, vertical, slash_offsets, counts):
    core = lax.axis_index("core")
    parity = lax.axis_index("zl")
    head = lax.axis_index("x") * lax.axis_size("zh") + lax.axis_index("zh")
    scalars = jnp.stack([core, (core == parity).astype(jnp.int32)]).astype(jnp.int32)

    tables = jnp.concatenate([vertical, slash_offsets, counts], axis=1)
    other_tables = lax.ppermute(tables, "core", SWAP)
    row = jnp.where(core == parity, tables[head], other_tables[head])
    nv, ns = vertical.shape[1], slash_offsets.shape[1]
    table = block_table(row[:nv], row[nv : nv + ns], row[nv + ns :], core)

    kept, sent = split_call(scalars, queries, key_rows, value_rows, out_grad)
    got = lax.ppermute(sent, "core", SWAP)
    kept = lax.dynamic_update_slice(kept, got[None], (1 - core, 0, 0, 0, 0))
    spread = kept.reshape(NBLOCKS, 2, BLK, HEAD_DIM)
    arrived = lax.all_to_all(spread, ORDER, split_axis=0, concat_axis=0, tiled=True)
    arrived = arrived.reshape(2, HALF, 2, BLK, HEAD_DIM)
    far_keys = lax.dynamic_index_in_dim(arrived, 1 - core, 0, keepdims=False)
    near_keys = lax.ppermute(far_keys, "core", SWAP)

    dq, partial, local = attend_call(scalars, table, arrived, near_keys)
    got_partial = lax.ppermute(partial, "core", SWAP)
    outgoing = join_call(scalars, dq, local, got_partial)
    outgoing = outgoing.reshape(NBLOCKS, BLK + BLK // 2, HEAD_DIM)
    returned = lax.all_to_all(outgoing, ORDER, split_axis=0, concat_axis=0, tiled=True)
    returned = returned.reshape(2, HALF, BLK + BLK // 2, HEAD_DIM)
    for_other = lax.dynamic_index_in_dim(returned, 1 - core, 0, keepdims=False)
    from_other = lax.ppermute(for_other, "core", SWAP)
    return tuple(merge_call(scalars, returned, from_other))


def solution(mesh):
    devices = mesh.devices
    fine = Mesh(devices.reshape(4, 4, 2, 8, 2), ("x", "zh", "zl", "y", "core"))
    rows = P(("y", "core", "x", "zh", "zl"), None)
    lists = P(("y", "core"), None)
    return jax.shard_map(
        body,
        mesh=fine,
        in_specs=(rows, rows, rows, rows, lists, lists, lists),
        out_specs=(rows, rows, rows),
        check_vma=False,
    )
```

```python
import functools

import jax
import jax.numpy as jnp
from jax import lax
from jax.experimental import pallas as pl
from jax.experimental.pallas import tpu as pltpu
from jax.sharding import Mesh
from jax.sharding import PartitionSpec as P

HEADS = 16
HEAD_DIM = 128
BLK = 128
NBLOCKS = 32
HALF = NBLOCKS // 2
SLOTS = 12
TOGETHER = 4
SCALE = HEAD_DIM ** (-0.5)
ORDER = ("zl", "x", "zh")
SWAP = [(0, 1), (1, 0)]
NEG = -1e30
VMEM_SPEC = pl.BlockSpec(memory_space=pltpu.VMEM)
ANY_SPEC = pl.BlockSpec(memory_space=pl.ANY)
HBM_SPEC = pl.BlockSpec(memory_space=pltpu.HBM)
SMEM_SPEC = pl.BlockSpec(memory_space=pltpu.SMEM)


def head_cols(h):
    return pl.ds(h * HEAD_DIM, HEAD_DIM)


def take_pair(first, second, target, sems):
    copies = [
        pltpu.make_async_copy(source.at[:, head_cols(h)], target.at[h, i], sems.at[2 * h + i])
        for h in range(HEADS)
        for i, source in enumerate((first, second))
    ]
    for copy in copies:
        copy.start()
    for copy in copies:
        copy.wait()


def sent_kernel(sc_ref, q_ref, k_ref, v_ref, d_ref, sent_ref, sems):
    @pl.when(sc_ref[1] == 1)
    def _():
        take_pair(k_ref, v_ref, sent_ref, sems)

    @pl.when(sc_ref[1] == 0)
    def _():
        take_pair(q_ref, d_ref, sent_ref, sems)


def kept_kernel(sc_ref, q_ref, k_ref, v_ref, d_ref, kept_ref, sems):
    mine = kept_ref.at[sc_ref[0]]

    @pl.when(sc_ref[1] == 1)
    def _():
        take_pair(q_ref, d_ref, mine, sems)

    @pl.when(sc_ref[1] == 0)
    def _():
        take_pair(k_ref, v_ref, mine, sems)


def pair_call(kernel, lead, grant, name, scalars, q, k, v, d):
    return pl.pallas_call(
        kernel,
        in_specs=[SMEM_SPEC] + [HBM_SPEC] * 4,
        out_specs=VMEM_SPEC,
        out_shape=jax.ShapeDtypeStruct(lead + (HEADS, 2, BLK, HEAD_DIM), jnp.bfloat16),
        scratch_shapes=[pltpu.SemaphoreType.DMA((2 * HEADS,))],
        cost_estimate=pl.CostEstimate(flops=0, transcendentals=0, bytes_accessed=4 * 2**20),
        compiler_params=pltpu.CompilerParams(vmem_limit_bytes=grant * 2**20),
        name=name,
    )(scalars, q, k, v, d)


def attend_kernel(
    sc_ref, tab_ref, y_ref, z_ref, dq_ref, send_ref, loc_ref, keys, values, dk_acc, dv_acc
):
    core = sc_ref[0]

    @pl.loop(0, HALF, unroll=4)
    def _(m):
        for t, k_tile, v_tile in (
            (m, z_ref[m, 0], z_ref[m, 1]),
            (HALF + m, y_ref[1 - core, m, 0], y_ref[1 - core, m, 1]),
        ):
            keys[t] = k_tile
            values[t] = v_tile
            dk_acc[t] = jnp.zeros((BLK, HEAD_DIM), jnp.float32)
            dv_acc[t] = jnp.zeros((BLK, HEAD_DIM), jnp.float32)

    @pl.loop(0, HALF // TOGETHER)
    def _(step):
        rows = [tab_ref[TOGETHER * step + r, SLOTS + 1] for r in range(TOGETHER)]
        counts = [tab_ref[m, SLOTS] for m in rows]
        pairs = (functools.reduce(jnp.maximum, counts) + 1) // 2

        for groups in range(1, SLOTS // 2 + 1):

            @pl.when(pairs == groups)
            def _(groups=groups):
                slots = range(2 * groups)
                scored = []
                for m, count in zip(rows, counts):
                    q = y_ref[core, m, 0]
                    d = y_ref[core, m, 1]
                    places = [tab_ref[m, a] for a in slots]
                    k_rows = jnp.concatenate([keys[t] for t in places], axis=0)
                    v_rows = jnp.concatenate([values[t] for t in places], axis=0)
                    s = jnp.dot(k_rows, q.T, preferred_element_type=jnp.float32)
                    g = jnp.dot(v_rows, d.T, preferred_element_type=jnp.float32)
                    s = jnp.concatenate(
                        [
                            s[a * BLK : (a + 1) * BLK] + jnp.where(a < count, 0.0, NEG)
                            for a in slots
                        ],
                        axis=0,
                    )
                    scored.append((m, q, d, places, k_rows, s, g))
                formed = []
                for m, q, d, places, k_rows, s, g in scored:
                    top = jnp.max(s, axis=0, keepdims=True)
                    e = jnp.exp((s - top) * SCALE)
                    inverse = 1.0 / jnp.sum(e, axis=0, keepdims=True)
                    delta = jnp.sum(e * g, axis=0, keepdims=True) * inverse
                    p = e * inverse
                    w = p.astype(jnp.bfloat16)
                    ds = (p * (g - delta)).astype(jnp.bfloat16)
                    formed.append((m, q, d, places, k_rows, w, ds))
                for m, q, d, places, k_rows, w, ds in formed:
                    for_keys = jnp.dot(ds, q, preferred_element_type=jnp.float32)
                    for_values = jnp.dot(w, d, preferred_element_type=jnp.float32)
                    for a in slots:
                        part = slice(a * BLK, (a + 1) * BLK)
                        dk_acc[places[a]] += for_keys[part]
                        dv_acc[places[a]] += for_values[part]
                    dq = lax.dot_general(
                        ds, k_rows, (((0,), (0,)), ((), ())), preferred_element_type=jnp.float32
                    )
                    dq_ref[m] = (dq * SCALE).astype(jnp.bfloat16)

    hb = BLK // 2

    @pl.loop(0, HALF, unroll=4)
    def _(m):
        far = HALF + m
        send_ref[m, :BLK] = (dk_acc[m] * SCALE).astype(jnp.bfloat16)
        send_ref[m, BLK : BLK + hb] = dv_acc[m, hb:].astype(jnp.bfloat16)
        send_ref[m, BLK + hb :] = dv_acc[far, :hb].astype(jnp.bfloat16)
        loc_ref[m, :BLK] = dk_acc[far] * SCALE
        loc_ref[m, BLK : BLK + hb] = dv_acc[far, hb:]
        loc_ref[m, BLK + hb :] = dv_acc[m, :hb]


def attend_call(scalars, table, y, z):
    return pl.pallas_call(
        attend_kernel,
        in_specs=[SMEM_SPEC, SMEM_SPEC, VMEM_SPEC, VMEM_SPEC],
        out_specs=[VMEM_SPEC, VMEM_SPEC, VMEM_SPEC],
        out_shape=[
            jax.ShapeDtypeStruct((HALF, BLK, HEAD_DIM), jnp.bfloat16),
            jax.ShapeDtypeStruct((HALF, 2 * BLK, HEAD_DIM), jnp.bfloat16),
            jax.ShapeDtypeStruct((HALF, 2 * BLK, HEAD_DIM), jnp.float32),
        ],
        scratch_shapes=[
            pltpu.VMEM((NBLOCKS, BLK, HEAD_DIM), jnp.bfloat16),
            pltpu.VMEM((NBLOCKS, BLK, HEAD_DIM), jnp.bfloat16),
            pltpu.VMEM((NBLOCKS, BLK, HEAD_DIM), jnp.float32),
            pltpu.VMEM((NBLOCKS, BLK, HEAD_DIM), jnp.float32),
        ],
        compiler_params=pltpu.CompilerParams(vmem_limit_bytes=24 * 2**20),
        name="attend",
    )(scalars, table, y, z)


def join_kernel(sc_ref, dq_ref, loc_ref, got_ref, out_ref):
    core = sc_ref[0]
    hb = BLK // 2
    summed = (loc_ref[...] + got_ref[...].astype(jnp.float32)).astype(jnp.bfloat16)
    out_ref[core, :, :BLK] = dq_ref[...]
    out_ref[core, :, BLK:] = summed[:, BLK + hb :]
    out_ref[1 - core] = summed[:, : BLK + hb]


def join_call(scalars, dq, loc, got):
    return pl.pallas_call(
        join_kernel,
        in_specs=[SMEM_SPEC, VMEM_SPEC, VMEM_SPEC, VMEM_SPEC],
        out_specs=VMEM_SPEC,
        out_shape=jax.ShapeDtypeStruct((2, HALF, BLK + BLK // 2, HEAD_DIM), jnp.bfloat16),
        compiler_params=pltpu.CompilerParams(vmem_limit_bytes=10 * 2**20),
        name="join_partials",
    )(scalars, dq, loc, got)


def put_pair(source, wide, narrow, half, sems):
    hb = BLK // 2
    copies = []
    for h in range(HEADS):
        copies.append(
            pltpu.make_async_copy(
                source.at[h, pl.ds(0, BLK)], wide.at[:, head_cols(h)], sems.at[2 * h]
            )
        )
        copies.append(
            pltpu.make_async_copy(
                source.at[h, pl.ds(BLK, hb)],
                narrow.at[pl.ds(half * hb, hb), head_cols(h)],
                sems.at[2 * h + 1],
            )
        )
    for copy in copies:
        copy.start()
    for copy in copies:
        copy.wait()


def own_kernel(sc_ref, own_ref, dq_ref, dk_ref, dv_ref, sems):
    mine = own_ref.at[sc_ref[0]]

    @pl.when(sc_ref[1] == 1)
    def _():
        put_pair(mine, dq_ref, dv_ref, 0, sems)

    @pl.when(sc_ref[1] == 0)
    def _():
        put_pair(mine, dk_ref, dv_ref, 1, sems)


def other_kernel(sc_ref, got_ref, dq_in, dk_in, dv_in, dq_ref, dk_ref, dv_ref, sems):
    del dq_in, dk_in, dv_in

    @pl.when(sc_ref[1] == 1)
    def _():
        put_pair(got_ref, dk_ref, dv_ref, 1, sems)

    @pl.when(sc_ref[1] == 0)
    def _():
        put_pair(got_ref, dq_ref, dv_ref, 0, sems)


def place_call(kernel, name, scalars, part, so_far):
    shape = jax.ShapeDtypeStruct((BLK, HEADS * HEAD_DIM), jnp.bfloat16)
    return pl.pallas_call(
        kernel,
        in_specs=[SMEM_SPEC, ANY_SPEC] + [HBM_SPEC] * len(so_far),
        out_specs=[HBM_SPEC] * 3,
        out_shape=[shape] * 3,
        input_output_aliases={2 + i: i for i in range(len(so_far))},
        scratch_shapes=[pltpu.SemaphoreType.DMA((2 * HEADS,))],
        cost_estimate=pl.CostEstimate(flops=0, transcendentals=0, bytes_accessed=4 * 2**20),
        compiler_params=pltpu.CompilerParams(vmem_limit_bytes=4 * 2**20),
        name=name,
    )(scalars, part, *so_far)


def block_table(vert, slash, count, core):
    chosen = core + 2 * jnp.arange(HALF, dtype=jnp.int32)
    vert_index = jnp.broadcast_to(vert[None, :], (HALF, vert.shape[0]))
    vert_valid = jnp.broadcast_to(
        (jnp.arange(vert.shape[0], dtype=jnp.int32) < count[0])[None, :], vert_index.shape
    )
    slash_index = chosen[:, None] - slash[None, :]
    inside = (slash_index >= 0) & (slash_index < NBLOCKS)
    repeated = jnp.any(
        (vert_index[:, :, None] == slash_index[:, None, :]) & vert_valid[:, :, None], axis=1
    )
    slash_valid = (
        (jnp.arange(slash.shape[0], dtype=jnp.int32) < count[1])[None, :]
        & inside
        & jnp.logical_not(repeated)
    )
    index = jnp.concatenate([vert_index, slash_index], axis=1)
    valid = jnp.concatenate([vert_valid, slash_valid], axis=1)
    place = ((index & 1) ^ core) * HALF + (index >> 1)
    rank = jnp.cumsum(valid.astype(jnp.int32), axis=1) - 1
    lanes = jnp.arange(SLOTS, dtype=jnp.int32)
    hit = valid[:, :, None] & (rank[:, :, None] == lanes[None, None, :])
    packed = jnp.sum(jnp.where(hit, place[:, :, None], 0), axis=1)
    total = jnp.sum(valid.astype(jnp.int32), axis=1, keepdims=True)
    m = jnp.arange(HALF, dtype=jnp.int32)
    ahead = (total[None, :, 0] > total) | ((total[None, :, 0] == total) & (m[None, :] < m[:, None]))
    rank_of = jnp.sum(ahead.astype(jnp.int32), axis=1)
    order = jnp.sum(jnp.where(rank_of[None, :] == m[:, None], m[None, :], 0), axis=1, keepdims=True)
    return jnp.concatenate([packed, total, order], axis=1)


def body(queries, key_rows, value_rows, out_grad, vertical, slash_offsets, counts):
    core = lax.axis_index("core")
    parity = lax.axis_index("zl")
    head = lax.axis_index("x") * lax.axis_size("zh") + lax.axis_index("zh")
    scalars = jnp.stack([core, (core == parity).astype(jnp.int32)]).astype(jnp.int32)

    tables = jnp.concatenate([vertical, slash_offsets, counts], axis=1)
    other_tables = lax.ppermute(tables, "core", SWAP)
    row = jnp.where(core == parity, tables[head], other_tables[head])
    nv, ns = vertical.shape[1], slash_offsets.shape[1]
    table = block_table(row[:nv], row[nv : nv + ns], row[nv + ns :], core)

    rows = tuple(
        pltpu.with_memory_space_constraint(x, pltpu.HBM)
        for x in (queries, key_rows, value_rows, out_grad)
    )
    sent = pair_call(sent_kernel, (), 4, "take_sent", scalars, *rows)
    got = lax.ppermute(sent, "core", SWAP)
    kept = pair_call(kept_kernel, (2,), 60, "take_kept", scalars, *rows)
    kept = lax.dynamic_update_slice(kept, got[None], (1 - core, 0, 0, 0, 0))
    spread = kept.reshape(NBLOCKS, 2, BLK, HEAD_DIM)
    arrived = lax.all_to_all(spread, ORDER, split_axis=0, concat_axis=0, tiled=True)
    arrived = arrived.reshape(2, HALF, 2, BLK, HEAD_DIM)
    far_keys = lax.dynamic_index_in_dim(arrived, 1 - core, 0, keepdims=False)
    near_keys = lax.ppermute(far_keys, "core", SWAP)

    dq, partial, local = attend_call(scalars, table, arrived, near_keys)
    got_partial = lax.ppermute(partial, "core", SWAP)
    outgoing = join_call(scalars, dq, local, got_partial)
    outgoing = outgoing.reshape(NBLOCKS, BLK + BLK // 2, HEAD_DIM)
    returned = lax.all_to_all(outgoing, ORDER, split_axis=0, concat_axis=0, tiled=True)
    returned = returned.reshape(2, HALF, BLK + BLK // 2, HEAD_DIM)
    for_other = lax.dynamic_index_in_dim(returned, 1 - core, 0, keepdims=False)
    from_other = lax.ppermute(for_other, "core", SWAP)
    so_far = place_call(own_kernel, "place_own", scalars, returned, ())
    return tuple(place_call(other_kernel, "place_other", scalars, from_other, so_far))


def solution(mesh):
    devices = mesh.devices
    fine = Mesh(devices.reshape(4, 4, 2, 8, 2), ("x", "zh", "zl", "y", "core"))
    rows = P(("y", "core", "x", "zh", "zl"), None)
    lists = P(("y", "core"), None)
    return jax.shard_map(
        body,
        mesh=fine,
        in_specs=(rows, rows, rows, rows, lists, lists, lists),
        out_specs=(rows, rows, rows),
        check_vma=False,
    )
```

```python
import functools

import jax
import jax.numpy as jnp
from jax import lax
from jax.experimental import pallas as pl
from jax.experimental.pallas import tpu as pltpu
from jax.sharding import Mesh
from jax.sharding import PartitionSpec as P

HEADS = 16
HEAD_DIM = 128
BLK = 128
NBLOCKS = 32
HALF = NBLOCKS // 2
SLOTS = 12
TOGETHER = 4
SCALE = HEAD_DIM ** (-0.5)
ORDER = ("zl", "x", "zh")
SWAP = [(0, 1), (1, 0)]
NEG = -1e30
VMEM_SPEC = pl.BlockSpec(memory_space=pltpu.VMEM)
ANY_SPEC = pl.BlockSpec(memory_space=pl.ANY)
HBM_SPEC = pl.BlockSpec(memory_space=pltpu.HBM)
SMEM_SPEC = pl.BlockSpec(memory_space=pltpu.SMEM)


CHUNK = 32


def take_pair(first, second, target, rows_buf, sems):
    parts = [
        (i, r, source)
        for r in range(0, BLK, CHUNK)
        for i, source in enumerate((first, second))
    ]
    copies = [
        pltpu.make_async_copy(
            source.at[pl.ds(r, CHUNK)], rows_buf.at[i, pl.ds(r, CHUNK)], sems.at[n]
        )
        for n, (i, r, source) in enumerate(parts)
    ]
    for copy in copies:
        copy.start()
    for copy, (i, r, _) in zip(copies, parts):
        copy.wait()
        for h in range(HEADS):
            target[h, i, r : r + CHUNK] = rows_buf[
                i, r : r + CHUNK, h * HEAD_DIM : (h + 1) * HEAD_DIM
            ]


def sent_kernel(sc_ref, q_ref, k_ref, v_ref, d_ref, sent_ref, rows_buf, sems):
    @pl.when(sc_ref[1] == 1)
    def _():
        take_pair(k_ref, v_ref, sent_ref, rows_buf, sems)

    @pl.when(sc_ref[1] == 0)
    def _():
        take_pair(q_ref, d_ref, sent_ref, rows_buf, sems)


def kept_kernel(sc_ref, q_ref, k_ref, v_ref, d_ref, kept_ref, rows_buf, sems):
    @pl.when(sc_ref[1] == 1)
    def _():
        take_pair(q_ref, d_ref, kept_ref, rows_buf, sems)

    @pl.when(sc_ref[1] == 0)
    def _():
        take_pair(k_ref, v_ref, kept_ref, rows_buf, sems)


def pair_call(kernel, name, scalars, q, k, v, d):
    return pl.pallas_call(
        kernel,
        in_specs=[SMEM_SPEC] + [HBM_SPEC] * 4,
        out_specs=VMEM_SPEC,
        out_shape=jax.ShapeDtypeStruct((HEADS, 2, BLK, HEAD_DIM), jnp.bfloat16),
        scratch_shapes=[
            pltpu.VMEM((2, BLK, HEADS * HEAD_DIM), jnp.bfloat16),
            pltpu.SemaphoreType.DMA((2 * BLK // CHUNK,)),
        ],
        cost_estimate=pl.CostEstimate(flops=0, transcendentals=0, bytes_accessed=4 * 2**20),
        compiler_params=pltpu.CompilerParams(vmem_limit_bytes=4 * 2**20),
        name=name,
    )(scalars, q, k, v, d)


def attend_kernel(
    sc_ref, tab_ref, y_ref, z_ref, dq_ref, send_ref, loc_ref, keys, values, dk_acc, dv_acc
):
    core = sc_ref[0]

    @pl.loop(0, HALF, unroll=4)
    def _(m):
        for t, k_tile, v_tile in (
            (m, z_ref[m, 0], z_ref[m, 1]),
            (HALF + m, y_ref[1 - core, m, 0], y_ref[1 - core, m, 1]),
        ):
            keys[t] = k_tile
            values[t] = v_tile
            dk_acc[t] = jnp.zeros((BLK, HEAD_DIM), jnp.float32)
            dv_acc[t] = jnp.zeros((BLK, HEAD_DIM), jnp.float32)

    @pl.loop(0, HALF // TOGETHER)
    def _(step):
        rows = [tab_ref[TOGETHER * step + r, SLOTS + 1] for r in range(TOGETHER)]
        counts = [tab_ref[m, SLOTS] for m in rows]
        pairs = (functools.reduce(jnp.maximum, counts) + 1) // 2

        for groups in range(1, SLOTS // 2 + 1):

            @pl.when(pairs == groups)
            def _(groups=groups):
                slots = range(2 * groups)
                scored = []
                for m, count in zip(rows, counts):
                    q = y_ref[core, m, 0]
                    d = y_ref[core, m, 1]
                    places = [tab_ref[m, a] for a in slots]
                    k_rows = jnp.concatenate([keys[t] for t in places], axis=0)
                    v_rows = jnp.concatenate([values[t] for t in places], axis=0)
                    s = jnp.dot(k_rows, q.T, preferred_element_type=jnp.float32)
                    g = jnp.dot(v_rows, d.T, preferred_element_type=jnp.float32)
                    s = jnp.concatenate(
                        [
                            s[a * BLK : (a + 1) * BLK] + jnp.where(a < count, 0.0, NEG)
                            for a in slots
                        ],
                        axis=0,
                    )
                    scored.append((m, q, d, places, k_rows, s, g))
                formed = []
                for m, q, d, places, k_rows, s, g in scored:
                    top = jnp.max(s, axis=0, keepdims=True)
                    e = jnp.exp((s - top) * SCALE)
                    inverse = 1.0 / jnp.sum(e, axis=0, keepdims=True)
                    delta = jnp.sum(e * g, axis=0, keepdims=True) * inverse
                    p = e * inverse
                    w = p.astype(jnp.bfloat16)
                    ds = (p * (g - delta)).astype(jnp.bfloat16)
                    formed.append((m, q, d, places, k_rows, w, ds))
                for m, q, d, places, k_rows, w, ds in formed:
                    for_keys = jnp.dot(ds, q, preferred_element_type=jnp.float32)
                    for_values = jnp.dot(w, d, preferred_element_type=jnp.float32)
                    for a in slots:
                        part = slice(a * BLK, (a + 1) * BLK)
                        dk_acc[places[a]] += for_keys[part]
                        dv_acc[places[a]] += for_values[part]
                    dq = lax.dot_general(
                        ds, k_rows, (((0,), (0,)), ((), ())), preferred_element_type=jnp.float32
                    )
                    dq_ref[m] = (dq * SCALE).astype(jnp.bfloat16)

    hb = BLK // 2

    @pl.loop(0, HALF, unroll=4)
    def _(m):
        far = HALF + m
        send_ref[m, :BLK] = (dk_acc[m] * SCALE).astype(jnp.bfloat16)
        send_ref[m, BLK : BLK + hb] = dv_acc[m, hb:].astype(jnp.bfloat16)
        send_ref[m, BLK + hb :] = dv_acc[far, :hb].astype(jnp.bfloat16)
        loc_ref[m, :BLK] = dk_acc[far] * SCALE
        loc_ref[m, BLK : BLK + hb] = dv_acc[far, hb:]
        loc_ref[m, BLK + hb :] = dv_acc[m, :hb]


def attend_call(scalars, table, y, z):
    return pl.pallas_call(
        attend_kernel,
        in_specs=[SMEM_SPEC, SMEM_SPEC, VMEM_SPEC, VMEM_SPEC],
        out_specs=[VMEM_SPEC, VMEM_SPEC, VMEM_SPEC],
        out_shape=[
            jax.ShapeDtypeStruct((HALF, BLK, HEAD_DIM), jnp.bfloat16),
            jax.ShapeDtypeStruct((HALF, 2 * BLK, HEAD_DIM), jnp.bfloat16),
            jax.ShapeDtypeStruct((HALF, 2 * BLK, HEAD_DIM), jnp.float32),
        ],
        scratch_shapes=[
            pltpu.VMEM((NBLOCKS, BLK, HEAD_DIM), jnp.bfloat16),
            pltpu.VMEM((NBLOCKS, BLK, HEAD_DIM), jnp.bfloat16),
            pltpu.VMEM((NBLOCKS, BLK, HEAD_DIM), jnp.float32),
            pltpu.VMEM((NBLOCKS, BLK, HEAD_DIM), jnp.float32),
        ],
        compiler_params=pltpu.CompilerParams(vmem_limit_bytes=24 * 2**20),
        name="attend",
    )(scalars, table, y, z)


def join_kernel(sc_ref, dq_ref, loc_ref, got_ref, out_ref):
    core = sc_ref[0]
    hb = BLK // 2
    summed = (loc_ref[...] + got_ref[...].astype(jnp.float32)).astype(jnp.bfloat16)
    out_ref[core, :, :BLK] = dq_ref[...]
    out_ref[core, :, BLK:] = summed[:, BLK + hb :]
    out_ref[1 - core] = summed[:, : BLK + hb]


def join_call(scalars, dq, loc, got):
    return pl.pallas_call(
        join_kernel,
        in_specs=[SMEM_SPEC, VMEM_SPEC, VMEM_SPEC, VMEM_SPEC],
        out_specs=VMEM_SPEC,
        out_shape=jax.ShapeDtypeStruct((2, HALF, BLK + BLK // 2, HEAD_DIM), jnp.bfloat16),
        compiler_params=pltpu.CompilerParams(vmem_limit_bytes=10 * 2**20),
        name="join_partials",
    )(scalars, dq, loc, got)


def put_pair(source, wide, narrow, half, wide_buf, narrow_buf, sems):
    hb = BLK // 2
    copies = []

    def fill(buf, target, first_row, buf_row, target_row, n):
        for h in range(HEADS):
            buf[buf_row : buf_row + CHUNK, h * HEAD_DIM : (h + 1) * HEAD_DIM] = source[
                h, first_row : first_row + CHUNK
            ]
        copy = pltpu.make_async_copy(
            buf.at[pl.ds(buf_row, CHUNK)], target.at[pl.ds(target_row, CHUNK)], sems.at[n]
        )
        copy.start()
        copies.append(copy)

    for r in range(0, BLK, CHUNK):
        fill(wide_buf, wide, r, r, r, len(copies))
    for r in range(0, hb, CHUNK):
        fill(narrow_buf, narrow, BLK + r, r, half * hb + r, len(copies))
    for copy in copies:
        copy.wait()


def own_kernel(sc_ref, own_ref, dq_ref, dk_ref, dv_ref, *bufs):
    mine = own_ref.at[sc_ref[0]]

    @pl.when(sc_ref[1] == 1)
    def _():
        put_pair(mine, dq_ref, dv_ref, 0, *bufs)

    @pl.when(sc_ref[1] == 0)
    def _():
        put_pair(mine, dk_ref, dv_ref, 1, *bufs)


def other_kernel(sc_ref, got_ref, dq_in, dk_in, dv_in, dq_ref, dk_ref, dv_ref, *bufs):
    del dq_in, dk_in, dv_in

    @pl.when(sc_ref[1] == 1)
    def _():
        put_pair(got_ref, dk_ref, dv_ref, 1, *bufs)

    @pl.when(sc_ref[1] == 0)
    def _():
        put_pair(got_ref, dq_ref, dv_ref, 0, *bufs)


def place_call(kernel, name, scalars, part, so_far):
    shape = jax.ShapeDtypeStruct((BLK, HEADS * HEAD_DIM), jnp.bfloat16)
    return pl.pallas_call(
        kernel,
        in_specs=[SMEM_SPEC, VMEM_SPEC] + [HBM_SPEC] * len(so_far),
        out_specs=[HBM_SPEC] * 3,
        out_shape=[shape] * 3,
        input_output_aliases={2 + i: i for i in range(len(so_far))},
        scratch_shapes=[
            pltpu.VMEM((BLK, HEADS * HEAD_DIM), jnp.bfloat16),
            pltpu.VMEM((BLK // 2, HEADS * HEAD_DIM), jnp.bfloat16),
            pltpu.SemaphoreType.DMA((6,)),
        ],
        cost_estimate=pl.CostEstimate(flops=0, transcendentals=0, bytes_accessed=4 * 2**20),
        compiler_params=pltpu.CompilerParams(vmem_limit_bytes=4 * 2**20),
        name=name,
    )(scalars, part, *so_far)


def block_table(vert, slash, count, core):
    chosen = core + 2 * jnp.arange(HALF, dtype=jnp.int32)
    vert_index = jnp.broadcast_to(vert[None, :], (HALF, vert.shape[0]))
    vert_valid = jnp.broadcast_to(
        (jnp.arange(vert.shape[0], dtype=jnp.int32) < count[0])[None, :], vert_index.shape
    )
    slash_index = chosen[:, None] - slash[None, :]
    inside = (slash_index >= 0) & (slash_index < NBLOCKS)
    repeated = jnp.any(
        (vert_index[:, :, None] == slash_index[:, None, :]) & vert_valid[:, :, None], axis=1
    )
    slash_valid = (
        (jnp.arange(slash.shape[0], dtype=jnp.int32) < count[1])[None, :]
        & inside
        & jnp.logical_not(repeated)
    )
    index = jnp.concatenate([vert_index, slash_index], axis=1)
    valid = jnp.concatenate([vert_valid, slash_valid], axis=1)
    place = ((index & 1) ^ core) * HALF + (index >> 1)
    rank = jnp.cumsum(valid.astype(jnp.int32), axis=1) - 1
    lanes = jnp.arange(SLOTS, dtype=jnp.int32)
    hit = valid[:, :, None] & (rank[:, :, None] == lanes[None, None, :])
    packed = jnp.sum(jnp.where(hit, place[:, :, None], 0), axis=1)
    total = jnp.sum(valid.astype(jnp.int32), axis=1, keepdims=True)
    m = jnp.arange(HALF, dtype=jnp.int32)
    ahead = (total[None, :, 0] > total) | ((total[None, :, 0] == total) & (m[None, :] < m[:, None]))
    rank_of = jnp.sum(ahead.astype(jnp.int32), axis=1)
    order = jnp.sum(jnp.where(rank_of[None, :] == m[:, None], m[None, :], 0), axis=1, keepdims=True)
    return jnp.concatenate([packed, total, order], axis=1)


def body(queries, key_rows, value_rows, out_grad, vertical, slash_offsets, counts):
    core = lax.axis_index("core")
    parity = lax.axis_index("zl")
    head = lax.axis_index("x") * lax.axis_size("zh") + lax.axis_index("zh")
    scalars = jnp.stack([core, (core == parity).astype(jnp.int32)]).astype(jnp.int32)

    tables = jnp.concatenate([vertical, slash_offsets, counts], axis=1)
    other_tables = lax.ppermute(tables, "core", SWAP)
    row = jnp.where(core == parity, tables[head], other_tables[head])
    nv, ns = vertical.shape[1], slash_offsets.shape[1]
    table = block_table(row[:nv], row[nv : nv + ns], row[nv + ns :], core)

    rows = tuple(
        pltpu.with_memory_space_constraint(x, pltpu.HBM)
        for x in (queries, key_rows, value_rows, out_grad)
    )
    sent = pair_call(sent_kernel, "take_sent", scalars, *rows)
    got = lax.ppermute(sent, "core", SWAP)
    kept = pair_call(kept_kernel, "take_kept", scalars, *rows)
    own_document = jnp.arange(2, dtype=jnp.int32).reshape(2, 1, 1, 1, 1) == core
    spread = jnp.where(own_document, kept[None], got[None])
    spread = spread.reshape(NBLOCKS, 2, BLK, HEAD_DIM)
    arrived = lax.all_to_all(spread, ORDER, split_axis=0, concat_axis=0, tiled=True)
    arrived = arrived.reshape(2, HALF, 2, BLK, HEAD_DIM)
    far_keys = lax.dynamic_index_in_dim(arrived, 1 - core, 0, keepdims=False)
    near_keys = lax.ppermute(far_keys, "core", SWAP)

    dq, partial, local = attend_call(scalars, table, arrived, near_keys)
    got_partial = lax.ppermute(partial, "core", SWAP)
    outgoing = join_call(scalars, dq, local, got_partial)
    outgoing = outgoing.reshape(NBLOCKS, BLK + BLK // 2, HEAD_DIM)
    returned = lax.all_to_all(outgoing, ORDER, split_axis=0, concat_axis=0, tiled=True)
    returned = returned.reshape(2, HALF, BLK + BLK // 2, HEAD_DIM)
    for_other = lax.dynamic_index_in_dim(returned, 1 - core, 0, keepdims=False)
    from_other = lax.ppermute(for_other, "core", SWAP)
    so_far = place_call(own_kernel, "place_own", scalars, returned, ())
    return tuple(place_call(other_kernel, "place_other", scalars, from_other, so_far))


def solution(mesh):
    devices = mesh.devices
    fine = Mesh(devices.reshape(4, 4, 2, 8, 2), ("x", "zh", "zl", "y", "core"))
    rows = P(("y", "core", "x", "zh", "zl"), None)
    lists = P(("y", "core"), None)
    return jax.shard_map(
        body,
        mesh=fine,
        in_specs=(rows, rows, rows, rows, lists, lists, lists),
        out_specs=(rows, rows, rows),
        check_vma=False,
    )
```

```python
import functools

import jax
import jax.numpy as jnp
from jax import lax
from jax.experimental import pallas as pl
from jax.experimental.pallas import tpu as pltpu
from jax.sharding import Mesh
from jax.sharding import PartitionSpec as P

HEADS = 16
HEAD_DIM = 128
BLK = 128
NBLOCKS = 32
HALF = NBLOCKS // 2
SLOTS = 12
TOGETHER = 8
SCALE = HEAD_DIM ** (-0.5)
ORDER = ("zl", "x", "zh")
SWAP = [(0, 1), (1, 0)]
NEG = -1e30
VMEM_SPEC = pl.BlockSpec(memory_space=pltpu.VMEM)
ANY_SPEC = pl.BlockSpec(memory_space=pl.ANY)
HBM_SPEC = pl.BlockSpec(memory_space=pltpu.HBM)
SMEM_SPEC = pl.BlockSpec(memory_space=pltpu.SMEM)


CHUNK = 32


def take_pair(first, second, target, rows_buf, sems):
    parts = [
        (i, r, source)
        for r in range(0, BLK, CHUNK)
        for i, source in enumerate((first, second))
    ]
    copies = [
        pltpu.make_async_copy(
            source.at[pl.ds(r, CHUNK)], rows_buf.at[i, pl.ds(r, CHUNK)], sems.at[n]
        )
        for n, (i, r, source) in enumerate(parts)
    ]
    for copy in copies:
        copy.start()
    for copy, (i, r, _) in zip(copies, parts):
        copy.wait()
        for h in range(HEADS):
            target[h, i, r : r + CHUNK] = rows_buf[
                i, r : r + CHUNK, h * HEAD_DIM : (h + 1) * HEAD_DIM
            ]


def sent_kernel(sc_ref, q_ref, k_ref, v_ref, d_ref, sent_ref, rows_buf, sems):
    @pl.when(sc_ref[1] == 1)
    def _():
        take_pair(k_ref, v_ref, sent_ref, rows_buf, sems)

    @pl.when(sc_ref[1] == 0)
    def _():
        take_pair(q_ref, d_ref, sent_ref, rows_buf, sems)


def kept_kernel(sc_ref, q_ref, k_ref, v_ref, d_ref, kept_ref, rows_buf, sems):
    @pl.when(sc_ref[1] == 1)
    def _():
        take_pair(q_ref, d_ref, kept_ref, rows_buf, sems)

    @pl.when(sc_ref[1] == 0)
    def _():
        take_pair(k_ref, v_ref, kept_ref, rows_buf, sems)


def pair_call(kernel, name, scalars, q, k, v, d):
    return pl.pallas_call(
        kernel,
        in_specs=[SMEM_SPEC] + [HBM_SPEC] * 4,
        out_specs=VMEM_SPEC,
        out_shape=jax.ShapeDtypeStruct((HEADS, 2, BLK, HEAD_DIM), jnp.bfloat16),
        scratch_shapes=[
            pltpu.VMEM((2, BLK, HEADS * HEAD_DIM), jnp.bfloat16),
            pltpu.SemaphoreType.DMA((2 * BLK // CHUNK,)),
        ],
        cost_estimate=pl.CostEstimate(flops=0, transcendentals=0, bytes_accessed=4 * 2**20),
        compiler_params=pltpu.CompilerParams(vmem_limit_bytes=4 * 2**20),
        name=name,
    )(scalars, q, k, v, d)


def attend_kernel(
    sc_ref, tab_ref, y_ref, z_ref, dq_ref, send_ref, loc_ref, keys, values, dk_acc, dv_acc
):
    core = sc_ref[0]

    @pl.loop(0, HALF, unroll=4)
    def _(m):
        for t, k_tile, v_tile in (
            (m, z_ref[m, 0], z_ref[m, 1]),
            (HALF + m, y_ref[1 - core, m, 0], y_ref[1 - core, m, 1]),
        ):
            keys[t] = k_tile
            values[t] = v_tile
            dk_acc[t] = jnp.zeros((BLK, HEAD_DIM), jnp.float32)
            dv_acc[t] = jnp.zeros((BLK, HEAD_DIM), jnp.float32)

    @pl.loop(0, HALF // TOGETHER)
    def _(step):
        rows = [tab_ref[TOGETHER * step + r, SLOTS + 1] for r in range(TOGETHER)]
        counts = [tab_ref[m, SLOTS] for m in rows]
        pairs = (functools.reduce(jnp.maximum, counts) + 1) // 2

        for groups in range(1, SLOTS // 2 + 1):

            @pl.when(pairs == groups)
            def _(groups=groups):
                slots = range(2 * groups)

                def score(r):
                    m, count = rows[r], counts[r]
                    q = y_ref[core, m, 0]
                    d = y_ref[core, m, 1]
                    places = [tab_ref[m, a] for a in slots]
                    k_rows = jnp.concatenate([keys[t] for t in places], axis=0)
                    v_rows = jnp.concatenate([values[t] for t in places], axis=0)
                    s = jnp.dot(k_rows, q.T, preferred_element_type=jnp.float32)
                    g = jnp.dot(v_rows, d.T, preferred_element_type=jnp.float32)
                    s = jnp.concatenate(
                        [
                            s[a * BLK : (a + 1) * BLK] + jnp.where(a < count, 0.0, NEG)
                            for a in slots
                        ],
                        axis=0,
                    )
                    return m, q, d, places, k_rows, s, g

                def form(m, q, d, places, k_rows, s, g):
                    top = jnp.max(s, axis=0, keepdims=True)
                    e = jnp.exp((s - top) * SCALE)
                    inverse = 1.0 / jnp.sum(e, axis=0, keepdims=True)
                    delta = jnp.sum(e * g, axis=0, keepdims=True) * inverse
                    p = e * inverse
                    w = p.astype(jnp.bfloat16)
                    ds = (p * (g - delta)).astype(jnp.bfloat16)
                    return m, q, d, places, k_rows, w, ds

                def spread(m, q, d, places, k_rows, w, ds):
                    for_keys = jnp.dot(ds, q, preferred_element_type=jnp.float32)
                    for_values = jnp.dot(w, d, preferred_element_type=jnp.float32)
                    for a in slots:
                        part = slice(a * BLK, (a + 1) * BLK)
                        dk_acc[places[a]] += for_keys[part]
                        dv_acc[places[a]] += for_values[part]
                    dq = lax.dot_general(
                        ds, k_rows, (((0,), (0,)), ((), ())), preferred_element_type=jnp.float32
                    )
                    dq_ref[m] = (dq * SCALE).astype(jnp.bfloat16)

                scored, formed = {}, {}
                for step_now in range(TOGETHER + 2):
                    if step_now < TOGETHER:
                        scored[step_now] = score(step_now)
                    if 0 <= step_now - 1 < TOGETHER:
                        formed[step_now - 1] = form(*scored.pop(step_now - 1))
                    if step_now >= 2:
                        spread(*formed.pop(step_now - 2))

    hb = BLK // 2

    @pl.loop(0, HALF, unroll=4)
    def _(m):
        far = HALF + m
        send_ref[m, :BLK] = (dk_acc[m] * SCALE).astype(jnp.bfloat16)
        send_ref[m, BLK : BLK + hb] = dv_acc[m, hb:].astype(jnp.bfloat16)
        send_ref[m, BLK + hb :] = dv_acc[far, :hb].astype(jnp.bfloat16)
        loc_ref[m, :BLK] = dk_acc[far] * SCALE
        loc_ref[m, BLK : BLK + hb] = dv_acc[far, hb:]
        loc_ref[m, BLK + hb :] = dv_acc[m, :hb]


def attend_call(scalars, table, y, z):
    return pl.pallas_call(
        attend_kernel,
        in_specs=[SMEM_SPEC, SMEM_SPEC, VMEM_SPEC, VMEM_SPEC],
        out_specs=[VMEM_SPEC, VMEM_SPEC, VMEM_SPEC],
        out_shape=[
            jax.ShapeDtypeStruct((HALF, BLK, HEAD_DIM), jnp.bfloat16),
            jax.ShapeDtypeStruct((HALF, 2 * BLK, HEAD_DIM), jnp.bfloat16),
            jax.ShapeDtypeStruct((HALF, 2 * BLK, HEAD_DIM), jnp.float32),
        ],
        scratch_shapes=[
            pltpu.VMEM((NBLOCKS, BLK, HEAD_DIM), jnp.bfloat16),
            pltpu.VMEM((NBLOCKS, BLK, HEAD_DIM), jnp.bfloat16),
            pltpu.VMEM((NBLOCKS, BLK, HEAD_DIM), jnp.float32),
            pltpu.VMEM((NBLOCKS, BLK, HEAD_DIM), jnp.float32),
        ],
        compiler_params=pltpu.CompilerParams(vmem_limit_bytes=24 * 2**20),
        name="attend",
    )(scalars, table, y, z)


def join_kernel(sc_ref, dq_ref, loc_ref, got_ref, out_ref):
    core = sc_ref[0]
    hb = BLK // 2
    summed = (loc_ref[...] + got_ref[...].astype(jnp.float32)).astype(jnp.bfloat16)
    out_ref[core, :, :BLK] = dq_ref[...]
    out_ref[core, :, BLK:] = summed[:, BLK + hb :]
    out_ref[1 - core] = summed[:, : BLK + hb]


def join_call(scalars, dq, loc, got):
    return pl.pallas_call(
        join_kernel,
        in_specs=[SMEM_SPEC, VMEM_SPEC, VMEM_SPEC, VMEM_SPEC],
        out_specs=VMEM_SPEC,
        out_shape=jax.ShapeDtypeStruct((2, HALF, BLK + BLK // 2, HEAD_DIM), jnp.bfloat16),
        compiler_params=pltpu.CompilerParams(vmem_limit_bytes=10 * 2**20),
        name="join_partials",
    )(scalars, dq, loc, got)


def put_pair(source, wide, narrow, half, wide_buf, narrow_buf, sems):
    hb = BLK // 2
    copies = []

    def fill(buf, target, first_row, buf_row, target_row, n):
        for h in range(HEADS):
            buf[buf_row : buf_row + CHUNK, h * HEAD_DIM : (h + 1) * HEAD_DIM] = source[
                h, first_row : first_row + CHUNK
            ]
        copy = pltpu.make_async_copy(
            buf.at[pl.ds(buf_row, CHUNK)], target.at[pl.ds(target_row, CHUNK)], sems.at[n]
        )
        copy.start()
        copies.append(copy)

    for r in range(0, BLK, CHUNK):
        fill(wide_buf, wide, r, r, r, len(copies))
    for r in range(0, hb, CHUNK):
        fill(narrow_buf, narrow, BLK + r, r, half * hb + r, len(copies))
    for copy in copies:
        copy.wait()


def own_kernel(sc_ref, own_ref, dq_ref, dk_ref, dv_ref, *bufs):
    mine = own_ref.at[sc_ref[0]]

    @pl.when(sc_ref[1] == 1)
    def _():
        put_pair(mine, dq_ref, dv_ref, 0, *bufs)

    @pl.when(sc_ref[1] == 0)
    def _():
        put_pair(mine, dk_ref, dv_ref, 1, *bufs)


def other_kernel(sc_ref, got_ref, dq_in, dk_in, dv_in, dq_ref, dk_ref, dv_ref, *bufs):
    del dq_in, dk_in, dv_in

    @pl.when(sc_ref[1] == 1)
    def _():
        put_pair(got_ref, dk_ref, dv_ref, 1, *bufs)

    @pl.when(sc_ref[1] == 0)
    def _():
        put_pair(got_ref, dq_ref, dv_ref, 0, *bufs)


def place_call(kernel, name, scalars, part, so_far):
    shape = jax.ShapeDtypeStruct((BLK, HEADS * HEAD_DIM), jnp.bfloat16)
    return pl.pallas_call(
        kernel,
        in_specs=[SMEM_SPEC, VMEM_SPEC] + [HBM_SPEC] * len(so_far),
        out_specs=[HBM_SPEC] * 3,
        out_shape=[shape] * 3,
        input_output_aliases={2 + i: i for i in range(len(so_far))},
        scratch_shapes=[
            pltpu.VMEM((BLK, HEADS * HEAD_DIM), jnp.bfloat16),
            pltpu.VMEM((BLK // 2, HEADS * HEAD_DIM), jnp.bfloat16),
            pltpu.SemaphoreType.DMA((6,)),
        ],
        cost_estimate=pl.CostEstimate(flops=0, transcendentals=0, bytes_accessed=4 * 2**20),
        compiler_params=pltpu.CompilerParams(vmem_limit_bytes=4 * 2**20),
        name=name,
    )(scalars, part, *so_far)


def block_table(vert, slash, count, core):
    chosen = core + 2 * jnp.arange(HALF, dtype=jnp.int32)
    vert_index = jnp.broadcast_to(vert[None, :], (HALF, vert.shape[0]))
    vert_valid = jnp.broadcast_to(
        (jnp.arange(vert.shape[0], dtype=jnp.int32) < count[0])[None, :], vert_index.shape
    )
    slash_index = chosen[:, None] - slash[None, :]
    inside = (slash_index >= 0) & (slash_index < NBLOCKS)
    repeated = jnp.any(
        (vert_index[:, :, None] == slash_index[:, None, :]) & vert_valid[:, :, None], axis=1
    )
    slash_valid = (
        (jnp.arange(slash.shape[0], dtype=jnp.int32) < count[1])[None, :]
        & inside
        & jnp.logical_not(repeated)
    )
    index = jnp.concatenate([vert_index, slash_index], axis=1)
    valid = jnp.concatenate([vert_valid, slash_valid], axis=1)
    place = ((index & 1) ^ core) * HALF + (index >> 1)
    rank = jnp.cumsum(valid.astype(jnp.int32), axis=1) - 1
    lanes = jnp.arange(SLOTS, dtype=jnp.int32)
    hit = valid[:, :, None] & (rank[:, :, None] == lanes[None, None, :])
    packed = jnp.sum(jnp.where(hit, place[:, :, None], 0), axis=1)
    total = jnp.sum(valid.astype(jnp.int32), axis=1, keepdims=True)
    m = jnp.arange(HALF, dtype=jnp.int32)
    ahead = (total[None, :, 0] > total) | ((total[None, :, 0] == total) & (m[None, :] < m[:, None]))
    rank_of = jnp.sum(ahead.astype(jnp.int32), axis=1)
    order = jnp.sum(jnp.where(rank_of[None, :] == m[:, None], m[None, :], 0), axis=1, keepdims=True)
    return jnp.concatenate([packed, total, order], axis=1)


def body(queries, key_rows, value_rows, out_grad, vertical, slash_offsets, counts):
    core = lax.axis_index("core")
    parity = lax.axis_index("zl")
    head = lax.axis_index("x") * lax.axis_size("zh") + lax.axis_index("zh")
    scalars = jnp.stack([core, (core == parity).astype(jnp.int32)]).astype(jnp.int32)

    tables = jnp.concatenate([vertical, slash_offsets, counts], axis=1)
    other_tables = lax.ppermute(tables, "core", SWAP)
    row = jnp.where(core == parity, tables[head], other_tables[head])
    nv, ns = vertical.shape[1], slash_offsets.shape[1]
    table = block_table(row[:nv], row[nv : nv + ns], row[nv + ns :], core)

    rows = tuple(
        pltpu.with_memory_space_constraint(x, pltpu.HBM)
        for x in (queries, key_rows, value_rows, out_grad)
    )
    sent = pair_call(sent_kernel, "take_sent", scalars, *rows)
    got = lax.ppermute(sent, "core", SWAP)
    kept = pair_call(kept_kernel, "take_kept", scalars, *rows)
    own_document = jnp.arange(2, dtype=jnp.int32).reshape(2, 1, 1, 1, 1) == core
    spread = jnp.where(own_document, kept[None], got[None])
    spread = spread.reshape(NBLOCKS, 2, BLK, HEAD_DIM)
    arrived = lax.all_to_all(spread, ORDER, split_axis=0, concat_axis=0, tiled=True)
    arrived = arrived.reshape(2, HALF, 2, BLK, HEAD_DIM)
    far_keys = lax.dynamic_index_in_dim(arrived, 1 - core, 0, keepdims=False)
    near_keys = lax.ppermute(far_keys, "core", SWAP)

    dq, partial, local = attend_call(scalars, table, arrived, near_keys)
    got_partial = lax.ppermute(partial, "core", SWAP)
    outgoing = join_call(scalars, dq, local, got_partial)
    outgoing = outgoing.reshape(NBLOCKS, BLK + BLK // 2, HEAD_DIM)
    returned = lax.all_to_all(outgoing, ORDER, split_axis=0, concat_axis=0, tiled=True)
    returned = returned.reshape(2, HALF, BLK + BLK // 2, HEAD_DIM)
    for_other = lax.dynamic_index_in_dim(returned, 1 - core, 0, keepdims=False)
    from_other = lax.ppermute(for_other, "core", SWAP)
    so_far = place_call(own_kernel, "place_own", scalars, returned, ())
    return tuple(place_call(other_kernel, "place_other", scalars, from_other, so_far))


def solution(mesh):
    devices = mesh.devices
    fine = Mesh(devices.reshape(4, 4, 2, 8, 2), ("x", "zh", "zl", "y", "core"))
    rows = P(("y", "core", "x", "zh", "zl"), None)
    lists = P(("y", "core"), None)
    return jax.shard_map(
        body,
        mesh=fine,
        in_specs=(rows, rows, rows, rows, lists, lists, lists),
        out_specs=(rows, rows, rows),
        check_vma=False,
    )
```

```python
import functools

import jax
import jax.numpy as jnp
from jax import lax
from jax.experimental import pallas as pl
from jax.experimental.pallas import tpu as pltpu
from jax.sharding import Mesh
from jax.sharding import PartitionSpec as P

HEADS = 16
HEAD_DIM = 128
BLK = 128
NBLOCKS = 32
HALF = NBLOCKS // 2
SLOTS = 12
TOGETHER = 8
SCALE = HEAD_DIM ** (-0.5)
ORDER = ("zl", "zh", "x")
SWAP = [(0, 1), (1, 0)]
NEG = -1e30
VMEM_SPEC = pl.BlockSpec(memory_space=pltpu.VMEM)
ANY_SPEC = pl.BlockSpec(memory_space=pl.ANY)
HBM_SPEC = pl.BlockSpec(memory_space=pltpu.HBM)
SMEM_SPEC = pl.BlockSpec(memory_space=pltpu.SMEM)


CHUNK = 32


def take_pair(first, second, target, rows_buf, sems):
    parts = [
        (i, r, source)
        for r in range(0, BLK, CHUNK)
        for i, source in enumerate((first, second))
    ]
    copies = [
        pltpu.make_async_copy(
            source.at[pl.ds(r, CHUNK)], rows_buf.at[i, pl.ds(r, CHUNK)], sems.at[n]
        )
        for n, (i, r, source) in enumerate(parts)
    ]
    for copy in copies:
        copy.start()
    for copy, (i, r, _) in zip(copies, parts):
        copy.wait()
        for h in range(HEADS):
            target[h, i, r : r + CHUNK] = rows_buf[
                i, r : r + CHUNK, h * HEAD_DIM : (h + 1) * HEAD_DIM
            ]


def sent_kernel(sc_ref, q_ref, k_ref, v_ref, d_ref, sent_ref, rows_buf, sems):
    @pl.when(sc_ref[1] == 1)
    def _():
        take_pair(k_ref, v_ref, sent_ref, rows_buf, sems)

    @pl.when(sc_ref[1] == 0)
    def _():
        take_pair(q_ref, d_ref, sent_ref, rows_buf, sems)


def kept_kernel(sc_ref, q_ref, k_ref, v_ref, d_ref, kept_ref, rows_buf, sems):
    @pl.when(sc_ref[1] == 1)
    def _():
        take_pair(q_ref, d_ref, kept_ref, rows_buf, sems)

    @pl.when(sc_ref[1] == 0)
    def _():
        take_pair(k_ref, v_ref, kept_ref, rows_buf, sems)


def pair_call(kernel, name, scalars, q, k, v, d):
    return pl.pallas_call(
        kernel,
        in_specs=[SMEM_SPEC] + [HBM_SPEC] * 4,
        out_specs=VMEM_SPEC,
        out_shape=jax.ShapeDtypeStruct((HEADS, 2, BLK, HEAD_DIM), jnp.bfloat16),
        scratch_shapes=[
            pltpu.VMEM((2, BLK, HEADS * HEAD_DIM), jnp.bfloat16),
            pltpu.SemaphoreType.DMA((2 * BLK // CHUNK,)),
        ],
        cost_estimate=pl.CostEstimate(flops=0, transcendentals=0, bytes_accessed=4 * 2**20),
        compiler_params=pltpu.CompilerParams(vmem_limit_bytes=4 * 2**20),
        name=name,
    )(scalars, q, k, v, d)


def attend_kernel(
    sc_ref, tab_ref, y_ref, z_ref, dq_ref, send_ref, loc_ref, keys, values, dk_acc, dv_acc
):
    core = sc_ref[0]

    @pl.loop(0, HALF, unroll=4)
    def _(m):
        for t, k_tile, v_tile in (
            (m, z_ref[m, 0], z_ref[m, 1]),
            (HALF + m, y_ref[1 - core, m, 0], y_ref[1 - core, m, 1]),
        ):
            keys[t] = k_tile
            values[t] = v_tile
            dk_acc[t] = jnp.zeros((BLK, HEAD_DIM), jnp.float32)
            dv_acc[t] = jnp.zeros((BLK, HEAD_DIM), jnp.float32)

    @pl.loop(0, HALF // TOGETHER)
    def _(step):
        rows = [tab_ref[TOGETHER * step + r, SLOTS + 1] for r in range(TOGETHER)]
        counts = [tab_ref[m, SLOTS] for m in rows]
        pairs = (functools.reduce(jnp.maximum, counts) + 1) // 2

        for groups in range(1, SLOTS // 2 + 1):

            @pl.when(pairs == groups)
            def _(groups=groups):
                slots = range(2 * groups)

                def score(r):
                    m, count = rows[r], counts[r]
                    q = y_ref[core, m, 0]
                    d = y_ref[core, m, 1]
                    places = [tab_ref[m, a] for a in slots]
                    k_rows = jnp.concatenate([keys[t] for t in places], axis=0)
                    v_rows = jnp.concatenate([values[t] for t in places], axis=0)
                    s = jnp.dot(k_rows, q.T, preferred_element_type=jnp.float32)
                    g = jnp.dot(v_rows, d.T, preferred_element_type=jnp.float32)
                    s = jnp.concatenate(
                        [
                            s[a * BLK : (a + 1) * BLK] + jnp.where(a < count, 0.0, NEG)
                            for a in slots
                        ],
                        axis=0,
                    )
                    return m, q, d, places, k_rows, s, g

                def form(m, q, d, places, k_rows, s, g):
                    top = jnp.max(s, axis=0, keepdims=True)
                    e = jnp.exp((s - top) * SCALE)
                    inverse = 1.0 / jnp.sum(e, axis=0, keepdims=True)
                    delta = jnp.sum(e * g, axis=0, keepdims=True) * inverse
                    p = e * inverse
                    w = p.astype(jnp.bfloat16)
                    ds = (p * (g - delta)).astype(jnp.bfloat16)
                    return m, q, d, places, k_rows, w, ds

                def spread(m, q, d, places, k_rows, w, ds):
                    for_keys = jnp.dot(ds, q, preferred_element_type=jnp.float32)
                    for_values = jnp.dot(w, d, preferred_element_type=jnp.float32)
                    for a in slots:
                        part = slice(a * BLK, (a + 1) * BLK)
                        dk_acc[places[a]] += for_keys[part]
                        dv_acc[places[a]] += for_values[part]
                    dq = lax.dot_general(
                        ds, k_rows, (((0,), (0,)), ((), ())), preferred_element_type=jnp.float32
                    )
                    dq_ref[m] = (dq * SCALE).astype(jnp.bfloat16)

                scored, formed = {}, {}
                for step_now in range(TOGETHER + 2):
                    if step_now < TOGETHER:
                        scored[step_now] = score(step_now)
                    if 0 <= step_now - 1 < TOGETHER:
                        formed[step_now - 1] = form(*scored.pop(step_now - 1))
                    if step_now >= 2:
                        spread(*formed.pop(step_now - 2))

    hb = BLK // 2

    @pl.loop(0, HALF, unroll=4)
    def _(m):
        far = HALF + m
        send_ref[m, :BLK] = (dk_acc[m] * SCALE).astype(jnp.bfloat16)
        send_ref[m, BLK : BLK + hb] = dv_acc[m, hb:].astype(jnp.bfloat16)
        send_ref[m, BLK + hb :] = dv_acc[far, :hb].astype(jnp.bfloat16)
        loc_ref[m, :BLK] = dk_acc[far] * SCALE
        loc_ref[m, BLK : BLK + hb] = dv_acc[far, hb:]
        loc_ref[m, BLK + hb :] = dv_acc[m, :hb]


def attend_call(scalars, table, y, z):
    return pl.pallas_call(
        attend_kernel,
        in_specs=[SMEM_SPEC, SMEM_SPEC, VMEM_SPEC, VMEM_SPEC],
        out_specs=[VMEM_SPEC, VMEM_SPEC, VMEM_SPEC],
        out_shape=[
            jax.ShapeDtypeStruct((HALF, BLK, HEAD_DIM), jnp.bfloat16),
            jax.ShapeDtypeStruct((HALF, 2 * BLK, HEAD_DIM), jnp.bfloat16),
            jax.ShapeDtypeStruct((HALF, 2 * BLK, HEAD_DIM), jnp.float32),
        ],
        scratch_shapes=[
            pltpu.VMEM((NBLOCKS, BLK, HEAD_DIM), jnp.bfloat16),
            pltpu.VMEM((NBLOCKS, BLK, HEAD_DIM), jnp.bfloat16),
            pltpu.VMEM((NBLOCKS, BLK, HEAD_DIM), jnp.float32),
            pltpu.VMEM((NBLOCKS, BLK, HEAD_DIM), jnp.float32),
        ],
        compiler_params=pltpu.CompilerParams(vmem_limit_bytes=24 * 2**20),
        name="attend",
    )(scalars, table, y, z)


def join_kernel(sc_ref, dq_ref, loc_ref, got_ref, out_ref):
    core = sc_ref[0]
    hb = BLK // 2
    summed = (loc_ref[...] + got_ref[...].astype(jnp.float32)).astype(jnp.bfloat16)
    out_ref[core, :, :BLK] = dq_ref[...]
    out_ref[core, :, BLK:] = summed[:, BLK + hb :]
    out_ref[1 - core] = summed[:, : BLK + hb]


def join_call(scalars, dq, loc, got):
    return pl.pallas_call(
        join_kernel,
        in_specs=[SMEM_SPEC, VMEM_SPEC, VMEM_SPEC, VMEM_SPEC],
        out_specs=VMEM_SPEC,
        out_shape=jax.ShapeDtypeStruct((2, HALF, BLK + BLK // 2, HEAD_DIM), jnp.bfloat16),
        compiler_params=pltpu.CompilerParams(vmem_limit_bytes=10 * 2**20),
        name="join_partials",
    )(scalars, dq, loc, got)


def put_pair(source, wide, narrow, half, wide_buf, narrow_buf, sems):
    hb = BLK // 2
    copies = []

    def fill(buf, target, first_row, buf_row, target_row, n):
        for h in range(HEADS):
            buf[buf_row : buf_row + CHUNK, h * HEAD_DIM : (h + 1) * HEAD_DIM] = source[
                h, first_row : first_row + CHUNK
            ]
        copy = pltpu.make_async_copy(
            buf.at[pl.ds(buf_row, CHUNK)], target.at[pl.ds(target_row, CHUNK)], sems.at[n]
        )
        copy.start()
        copies.append(copy)

    for r in range(0, BLK, CHUNK):
        fill(wide_buf, wide, r, r, r, len(copies))
    for r in range(0, hb, CHUNK):
        fill(narrow_buf, narrow, BLK + r, r, half * hb + r, len(copies))
    for copy in copies:
        copy.wait()


def own_kernel(sc_ref, own_ref, dq_ref, dk_ref, dv_ref, *bufs):
    mine = own_ref.at[sc_ref[0]]

    @pl.when(sc_ref[1] == 1)
    def _():
        put_pair(mine, dq_ref, dv_ref, 0, *bufs)

    @pl.when(sc_ref[1] == 0)
    def _():
        put_pair(mine, dk_ref, dv_ref, 1, *bufs)


def other_kernel(sc_ref, got_ref, dq_in, dk_in, dv_in, dq_ref, dk_ref, dv_ref, *bufs):
    del dq_in, dk_in, dv_in

    @pl.when(sc_ref[1] == 1)
    def _():
        put_pair(got_ref, dk_ref, dv_ref, 1, *bufs)

    @pl.when(sc_ref[1] == 0)
    def _():
        put_pair(got_ref, dq_ref, dv_ref, 0, *bufs)


def place_call(kernel, name, scalars, part, so_far):
    shape = jax.ShapeDtypeStruct((BLK, HEADS * HEAD_DIM), jnp.bfloat16)
    return pl.pallas_call(
        kernel,
        in_specs=[SMEM_SPEC, VMEM_SPEC] + [HBM_SPEC] * len(so_far),
        out_specs=[HBM_SPEC] * 3,
        out_shape=[shape] * 3,
        input_output_aliases={2 + i: i for i in range(len(so_far))},
        scratch_shapes=[
            pltpu.VMEM((BLK, HEADS * HEAD_DIM), jnp.bfloat16),
            pltpu.VMEM((BLK // 2, HEADS * HEAD_DIM), jnp.bfloat16),
            pltpu.SemaphoreType.DMA((6,)),
        ],
        cost_estimate=pl.CostEstimate(flops=0, transcendentals=0, bytes_accessed=4 * 2**20),
        compiler_params=pltpu.CompilerParams(vmem_limit_bytes=4 * 2**20),
        name=name,
    )(scalars, part, *so_far)


def turned(m):
    return ((m & 3) << 2) | ((m >> 2) & 3)


def block_table(vert, slash, count, core):
    chosen = core + 2 * turned(jnp.arange(HALF, dtype=jnp.int32))
    vert_index = jnp.broadcast_to(vert[None, :], (HALF, vert.shape[0]))
    vert_valid = jnp.broadcast_to(
        (jnp.arange(vert.shape[0], dtype=jnp.int32) < count[0])[None, :], vert_index.shape
    )
    slash_index = chosen[:, None] - slash[None, :]
    inside = (slash_index >= 0) & (slash_index < NBLOCKS)
    repeated = jnp.any(
        (vert_index[:, :, None] == slash_index[:, None, :]) & vert_valid[:, :, None], axis=1
    )
    slash_valid = (
        (jnp.arange(slash.shape[0], dtype=jnp.int32) < count[1])[None, :]
        & inside
        & jnp.logical_not(repeated)
    )
    index = jnp.concatenate([vert_index, slash_index], axis=1)
    valid = jnp.concatenate([vert_valid, slash_valid], axis=1)
    place = ((index & 1) ^ core) * HALF + turned(index >> 1)
    rank = jnp.cumsum(valid.astype(jnp.int32), axis=1) - 1
    lanes = jnp.arange(SLOTS, dtype=jnp.int32)
    hit = valid[:, :, None] & (rank[:, :, None] == lanes[None, None, :])
    packed = jnp.sum(jnp.where(hit, place[:, :, None], 0), axis=1)
    total = jnp.sum(valid.astype(jnp.int32), axis=1, keepdims=True)
    m = jnp.arange(HALF, dtype=jnp.int32)
    ahead = (total[None, :, 0] > total) | ((total[None, :, 0] == total) & (m[None, :] < m[:, None]))
    rank_of = jnp.sum(ahead.astype(jnp.int32), axis=1)
    order = jnp.sum(jnp.where(rank_of[None, :] == m[:, None], m[None, :], 0), axis=1, keepdims=True)
    return jnp.concatenate([packed, total, order], axis=1)


def body(queries, key_rows, value_rows, out_grad, vertical, slash_offsets, counts):
    core = lax.axis_index("core")
    parity = lax.axis_index("zl")
    head = lax.axis_index("zh") * lax.axis_size("x") + lax.axis_index("x")
    scalars = jnp.stack([core, (core == parity).astype(jnp.int32)]).astype(jnp.int32)

    tables = jnp.concatenate([vertical, slash_offsets, counts], axis=1)
    other_tables = lax.ppermute(tables, "core", SWAP)
    row = jnp.where(core == parity, tables[head], other_tables[head])
    nv, ns = vertical.shape[1], slash_offsets.shape[1]
    table = block_table(row[:nv], row[nv : nv + ns], row[nv + ns :], core)

    rows = tuple(
        pltpu.with_memory_space_constraint(x, pltpu.HBM)
        for x in (queries, key_rows, value_rows, out_grad)
    )
    sent = pair_call(sent_kernel, "take_sent", scalars, *rows)
    got = lax.ppermute(sent, "core", SWAP)
    kept = pair_call(kept_kernel, "take_kept", scalars, *rows)
    own_document = jnp.arange(2, dtype=jnp.int32).reshape(2, 1, 1, 1, 1) == core
    spread = jnp.where(own_document, kept[None], got[None])
    spread = spread.reshape(NBLOCKS, 2, BLK, HEAD_DIM)
    arrived = lax.all_to_all(spread, ORDER, split_axis=0, concat_axis=0, tiled=True)
    arrived = arrived.reshape(2, HALF, 2, BLK, HEAD_DIM)
    far_keys = lax.dynamic_index_in_dim(arrived, 1 - core, 0, keepdims=False)
    near_keys = lax.ppermute(far_keys, "core", SWAP)

    dq, partial, local = attend_call(scalars, table, arrived, near_keys)
    got_partial = lax.ppermute(partial, "core", SWAP)
    outgoing = join_call(scalars, dq, local, got_partial)
    outgoing = outgoing.reshape(NBLOCKS, BLK + BLK // 2, HEAD_DIM)
    returned = lax.all_to_all(outgoing, ORDER, split_axis=0, concat_axis=0, tiled=True)
    returned = returned.reshape(2, HALF, BLK + BLK // 2, HEAD_DIM)
    for_other = lax.dynamic_index_in_dim(returned, 1 - core, 0, keepdims=False)
    from_other = lax.ppermute(for_other, "core", SWAP)
    so_far = place_call(own_kernel, "place_own", scalars, returned, ())
    return tuple(place_call(other_kernel, "place_other", scalars, from_other, so_far))


def solution(mesh):
    devices = mesh.devices
    fine = Mesh(devices.reshape(4, 4, 2, 8, 2), ("x", "zh", "zl", "y", "core"))
    rows = P(("y", "core", "x", "zh", "zl"), None)
    lists = P(("y", "core"), None)
    return jax.shard_map(
        body,
        mesh=fine,
        in_specs=(rows, rows, rows, rows, lists, lists, lists),
        out_specs=(rows, rows, rows),
        check_vma=False,
    )
```

```python
import functools

import jax
import jax.numpy as jnp
from jax import lax
from jax.experimental import pallas as pl
from jax.experimental.pallas import tpu as pltpu
from jax.sharding import Mesh
from jax.sharding import PartitionSpec as P

HEADS = 16
HEAD_DIM = 128
BLK = 128
NBLOCKS = 32
HALF = NBLOCKS // 2
SLOTS = 12
TOGETHER = 8
SCALE = HEAD_DIM ** (-0.5)
ORDER = ("zl", "zh", "x")
SWAP = [(0, 1), (1, 0)]
NEG = -1e30
VMEM_SPEC = pl.BlockSpec(memory_space=pltpu.VMEM)
ANY_SPEC = pl.BlockSpec(memory_space=pl.ANY)
HBM_SPEC = pl.BlockSpec(memory_space=pltpu.HBM)
SMEM_SPEC = pl.BlockSpec(memory_space=pltpu.SMEM)


CHUNK = 16


def take_pair(first, second, target, rows_buf, sems):
    parts = [
        (i, r, source)
        for r in range(0, BLK, CHUNK)
        for i, source in enumerate((first, second))
    ]
    copies = [
        pltpu.make_async_copy(
            source.at[pl.ds(r, CHUNK)], rows_buf.at[i, pl.ds(r, CHUNK)], sems.at[n]
        )
        for n, (i, r, source) in enumerate(parts)
    ]
    for copy in copies:
        copy.start()
    for copy, (i, r, _) in zip(copies, parts):
        copy.wait()
        for h in range(HEADS):
            target[h, i, r : r + CHUNK] = rows_buf[
                i, r : r + CHUNK, h * HEAD_DIM : (h + 1) * HEAD_DIM
            ]


def sent_kernel(sc_ref, q_ref, k_ref, v_ref, d_ref, sent_ref, rows_buf, sems):
    @pl.when(sc_ref[1] == 1)
    def _():
        take_pair(k_ref, v_ref, sent_ref, rows_buf, sems)

    @pl.when(sc_ref[1] == 0)
    def _():
        take_pair(q_ref, d_ref, sent_ref, rows_buf, sems)


def kept_kernel(sc_ref, q_ref, k_ref, v_ref, d_ref, kept_ref, rows_buf, sems):
    @pl.when(sc_ref[1] == 1)
    def _():
        take_pair(q_ref, d_ref, kept_ref, rows_buf, sems)

    @pl.when(sc_ref[1] == 0)
    def _():
        take_pair(k_ref, v_ref, kept_ref, rows_buf, sems)


def pair_call(kernel, name, scalars, q, k, v, d):
    return pl.pallas_call(
        kernel,
        in_specs=[SMEM_SPEC] + [HBM_SPEC] * 4,
        out_specs=VMEM_SPEC,
        out_shape=jax.ShapeDtypeStruct((HEADS, 2, BLK, HEAD_DIM), jnp.bfloat16),
        scratch_shapes=[
            pltpu.VMEM((2, BLK, HEADS * HEAD_DIM), jnp.bfloat16),
            pltpu.SemaphoreType.DMA((2 * BLK // CHUNK,)),
        ],
        cost_estimate=pl.CostEstimate(flops=0, transcendentals=0, bytes_accessed=4 * 2**20),
        compiler_params=pltpu.CompilerParams(vmem_limit_bytes=4 * 2**20),
        name=name,
    )(scalars, q, k, v, d)


def attend_kernel(
    sc_ref, tab_ref, y_ref, z_ref, dq_ref, send_ref, loc_ref, keys, values, dk_acc, dv_acc
):
    core = sc_ref[0]

    @pl.loop(0, HALF, unroll=4)
    def _(m):
        for t, k_tile, v_tile in (
            (m, z_ref[m, 0], z_ref[m, 1]),
            (HALF + m, y_ref[1 - core, m, 0], y_ref[1 - core, m, 1]),
        ):
            keys[t] = k_tile
            values[t] = v_tile
            dk_acc[t] = jnp.zeros((BLK, HEAD_DIM), jnp.float32)
            dv_acc[t] = jnp.zeros((BLK, HEAD_DIM), jnp.float32)

    @pl.loop(0, HALF // TOGETHER)
    def _(step):
        rows = [tab_ref[TOGETHER * step + r, SLOTS + 1] for r in range(TOGETHER)]
        counts = [tab_ref[m, SLOTS] for m in rows]
        pairs = (functools.reduce(jnp.maximum, counts) + 1) // 2

        for groups in range(1, SLOTS // 2 + 1):

            @pl.when(pairs == groups)
            def _(groups=groups):
                slots = range(2 * groups)

                def score(r):
                    m, count = rows[r], counts[r]
                    q = y_ref[core, m, 0]
                    d = y_ref[core, m, 1]
                    places = [tab_ref[m, a] for a in slots]
                    k_rows = jnp.concatenate([keys[t] for t in places], axis=0)
                    v_rows = jnp.concatenate([values[t] for t in places], axis=0)
                    s = jnp.dot(k_rows, q.T, preferred_element_type=jnp.float32)
                    g = jnp.dot(v_rows, d.T, preferred_element_type=jnp.float32)
                    s = jnp.concatenate(
                        [
                            s[a * BLK : (a + 1) * BLK] + jnp.where(a < count, 0.0, NEG)
                            for a in slots
                        ],
                        axis=0,
                    )
                    return m, q, d, places, k_rows, s, g

                def form(m, q, d, places, k_rows, s, g):
                    top = jnp.max(s, axis=0, keepdims=True)
                    e = jnp.exp((s - top) * SCALE)
                    inverse = 1.0 / jnp.sum(e, axis=0, keepdims=True)
                    delta = jnp.sum(e * g, axis=0, keepdims=True) * inverse
                    p = e * inverse
                    w = p.astype(jnp.bfloat16)
                    ds = (p * (g - delta)).astype(jnp.bfloat16)
                    return m, q, d, places, k_rows, w, ds

                def spread(m, q, d, places, k_rows, w, ds):
                    for_keys = jnp.dot(ds, q, preferred_element_type=jnp.float32)
                    for_values = jnp.dot(w, d, preferred_element_type=jnp.float32)
                    for a in slots:
                        part = slice(a * BLK, (a + 1) * BLK)
                        dk_acc[places[a]] += for_keys[part]
                        dv_acc[places[a]] += for_values[part]
                    dq = lax.dot_general(
                        ds, k_rows, (((0,), (0,)), ((), ())), preferred_element_type=jnp.float32
                    )
                    dq_ref[m] = (dq * SCALE).astype(jnp.bfloat16)

                scored, formed = {}, {}
                for step_now in range(TOGETHER + 2):
                    if step_now < TOGETHER:
                        scored[step_now] = score(step_now)
                    if 0 <= step_now - 1 < TOGETHER:
                        formed[step_now - 1] = form(*scored.pop(step_now - 1))
                    if step_now >= 2:
                        spread(*formed.pop(step_now - 2))

    hb = BLK // 2

    @pl.loop(0, HALF, unroll=4)
    def _(m):
        far = HALF + m
        send_ref[m, :BLK] = (dk_acc[m] * SCALE).astype(jnp.bfloat16)
        send_ref[m, BLK : BLK + hb] = dv_acc[m, hb:].astype(jnp.bfloat16)
        send_ref[m, BLK + hb :] = dv_acc[far, :hb].astype(jnp.bfloat16)
        loc_ref[m, :BLK] = dk_acc[far] * SCALE
        loc_ref[m, BLK : BLK + hb] = dv_acc[far, hb:]
        loc_ref[m, BLK + hb :] = dv_acc[m, :hb]


def attend_call(scalars, table, y, z):
    return pl.pallas_call(
        attend_kernel,
        in_specs=[SMEM_SPEC, SMEM_SPEC, VMEM_SPEC, VMEM_SPEC],
        out_specs=[VMEM_SPEC, VMEM_SPEC, VMEM_SPEC],
        out_shape=[
            jax.ShapeDtypeStruct((HALF, BLK, HEAD_DIM), jnp.bfloat16),
            jax.ShapeDtypeStruct((HALF, 2 * BLK, HEAD_DIM), jnp.bfloat16),
            jax.ShapeDtypeStruct((HALF, 2 * BLK, HEAD_DIM), jnp.float32),
        ],
        scratch_shapes=[
            pltpu.VMEM((NBLOCKS, BLK, HEAD_DIM), jnp.bfloat16),
            pltpu.VMEM((NBLOCKS, BLK, HEAD_DIM), jnp.bfloat16),
            pltpu.VMEM((NBLOCKS, BLK, HEAD_DIM), jnp.float32),
            pltpu.VMEM((NBLOCKS, BLK, HEAD_DIM), jnp.float32),
        ],
        compiler_params=pltpu.CompilerParams(vmem_limit_bytes=24 * 2**20),
        name="attend",
    )(scalars, table, y, z)


def join_kernel(sc_ref, dq_ref, loc_ref, got_ref, out_ref):
    core = sc_ref[0]
    hb = BLK // 2
    summed = (loc_ref[...] + got_ref[...].astype(jnp.float32)).astype(jnp.bfloat16)
    out_ref[core, :, :BLK] = dq_ref[...]
    out_ref[core, :, BLK:] = summed[:, BLK + hb :]
    out_ref[1 - core] = summed[:, : BLK + hb]


def join_call(scalars, dq, loc, got):
    return pl.pallas_call(
        join_kernel,
        in_specs=[SMEM_SPEC, VMEM_SPEC, VMEM_SPEC, VMEM_SPEC],
        out_specs=VMEM_SPEC,
        out_shape=jax.ShapeDtypeStruct((2, HALF, BLK + BLK // 2, HEAD_DIM), jnp.bfloat16),
        compiler_params=pltpu.CompilerParams(vmem_limit_bytes=10 * 2**20),
        name="join_partials",
    )(scalars, dq, loc, got)


def put_pair(source, wide, narrow, half, wide_buf, narrow_buf, sems):
    hb = BLK // 2
    copies = []

    def fill(buf, target, first_row, buf_row, target_row, n):
        for h in range(HEADS):
            buf[buf_row : buf_row + CHUNK, h * HEAD_DIM : (h + 1) * HEAD_DIM] = source[
                h, first_row : first_row + CHUNK
            ]
        copy = pltpu.make_async_copy(
            buf.at[pl.ds(buf_row, CHUNK)], target.at[pl.ds(target_row, CHUNK)], sems.at[n]
        )
        copy.start()
        copies.append(copy)

    for r in range(0, BLK, CHUNK):
        fill(wide_buf, wide, r, r, r, len(copies))
    for r in range(0, hb, CHUNK):
        fill(narrow_buf, narrow, BLK + r, r, half * hb + r, len(copies))
    for copy in copies:
        copy.wait()


def own_kernel(sc_ref, own_ref, dq_ref, dk_ref, dv_ref, *bufs):
    mine = own_ref.at[sc_ref[0]]

    @pl.when(sc_ref[1] == 1)
    def _():
        put_pair(mine, dq_ref, dv_ref, 0, *bufs)

    @pl.when(sc_ref[1] == 0)
    def _():
        put_pair(mine, dk_ref, dv_ref, 1, *bufs)


def other_kernel(sc_ref, got_ref, dq_in, dk_in, dv_in, dq_ref, dk_ref, dv_ref, *bufs):
    del dq_in, dk_in, dv_in

    @pl.when(sc_ref[1] == 1)
    def _():
        put_pair(got_ref, dk_ref, dv_ref, 1, *bufs)

    @pl.when(sc_ref[1] == 0)
    def _():
        put_pair(got_ref, dq_ref, dv_ref, 0, *bufs)


def place_call(kernel, name, scalars, part, so_far):
    shape = jax.ShapeDtypeStruct((BLK, HEADS * HEAD_DIM), jnp.bfloat16)
    return pl.pallas_call(
        kernel,
        in_specs=[SMEM_SPEC, VMEM_SPEC] + [HBM_SPEC] * len(so_far),
        out_specs=[HBM_SPEC] * 3,
        out_shape=[shape] * 3,
        input_output_aliases={2 + i: i for i in range(len(so_far))},
        scratch_shapes=[
            pltpu.VMEM((BLK, HEADS * HEAD_DIM), jnp.bfloat16),
            pltpu.VMEM((BLK // 2, HEADS * HEAD_DIM), jnp.bfloat16),
            pltpu.SemaphoreType.DMA((12,)),
        ],
        cost_estimate=pl.CostEstimate(flops=0, transcendentals=0, bytes_accessed=4 * 2**20),
        compiler_params=pltpu.CompilerParams(vmem_limit_bytes=4 * 2**20),
        name=name,
    )(scalars, part, *so_far)


def turned(m):
    return ((m & 3) << 2) | ((m >> 2) & 3)


def block_table(vert, slash, count, core):
    chosen = core + 2 * turned(jnp.arange(HALF, dtype=jnp.int32))
    vert_index = jnp.broadcast_to(vert[None, :], (HALF, vert.shape[0]))
    vert_valid = jnp.broadcast_to(
        (jnp.arange(vert.shape[0], dtype=jnp.int32) < count[0])[None, :], vert_index.shape
    )
    slash_index = chosen[:, None] - slash[None, :]
    inside = (slash_index >= 0) & (slash_index < NBLOCKS)
    repeated = jnp.any(
        (vert_index[:, :, None] == slash_index[:, None, :]) & vert_valid[:, :, None], axis=1
    )
    slash_valid = (
        (jnp.arange(slash.shape[0], dtype=jnp.int32) < count[1])[None, :]
        & inside
        & jnp.logical_not(repeated)
    )
    index = jnp.concatenate([vert_index, slash_index], axis=1)
    valid = jnp.concatenate([vert_valid, slash_valid], axis=1)
    place = ((index & 1) ^ core) * HALF + turned(index >> 1)
    rank = jnp.cumsum(valid.astype(jnp.int32), axis=1) - 1
    lanes = jnp.arange(SLOTS, dtype=jnp.int32)
    hit = valid[:, :, None] & (rank[:, :, None] == lanes[None, None, :])
    packed = jnp.sum(jnp.where(hit, place[:, :, None], 0), axis=1)
    total = jnp.sum(valid.astype(jnp.int32), axis=1, keepdims=True)
    m = jnp.arange(HALF, dtype=jnp.int32)
    ahead = (total[None, :, 0] > total) | ((total[None, :, 0] == total) & (m[None, :] < m[:, None]))
    rank_of = jnp.sum(ahead.astype(jnp.int32), axis=1)
    order = jnp.sum(jnp.where(rank_of[None, :] == m[:, None], m[None, :], 0), axis=1, keepdims=True)
    return jnp.concatenate([packed, total, order], axis=1)


def body(queries, key_rows, value_rows, out_grad, vertical, slash_offsets, counts):
    core = lax.axis_index("core")
    parity = lax.axis_index("zl")
    head = lax.axis_index("zh") * lax.axis_size("x") + lax.axis_index("x")
    scalars = jnp.stack([core, (core == parity).astype(jnp.int32)]).astype(jnp.int32)

    tables = jnp.concatenate([vertical, slash_offsets, counts], axis=1)
    other_tables = lax.ppermute(tables, "core", SWAP)
    row = jnp.where(core == parity, tables[head], other_tables[head])
    nv, ns = vertical.shape[1], slash_offsets.shape[1]
    table = block_table(row[:nv], row[nv : nv + ns], row[nv + ns :], core)

    rows = tuple(
        pltpu.with_memory_space_constraint(x, pltpu.HBM)
        for x in (queries, key_rows, value_rows, out_grad)
    )
    sent = pair_call(sent_kernel, "take_sent", scalars, *rows)
    got = lax.ppermute(sent, "core", SWAP)
    kept = pair_call(kept_kernel, "take_kept", scalars, *rows)
    own_document = jnp.arange(2, dtype=jnp.int32).reshape(2, 1, 1, 1, 1) == core
    spread = jnp.where(own_document, kept[None], got[None])
    spread = spread.reshape(NBLOCKS, 2, BLK, HEAD_DIM)
    arrived = lax.all_to_all(spread, ORDER, split_axis=0, concat_axis=0, tiled=True)
    arrived = arrived.reshape(2, HALF, 2, BLK, HEAD_DIM)
    far_keys = lax.dynamic_index_in_dim(arrived, 1 - core, 0, keepdims=False)
    near_keys = lax.ppermute(far_keys, "core", SWAP)

    dq, partial, local = attend_call(scalars, table, arrived, near_keys)
    got_partial = lax.ppermute(partial, "core", SWAP)
    outgoing = join_call(scalars, dq, local, got_partial)
    outgoing = outgoing.reshape(NBLOCKS, BLK + BLK // 2, HEAD_DIM)
    returned = lax.all_to_all(outgoing, ORDER, split_axis=0, concat_axis=0, tiled=True)
    returned = returned.reshape(2, HALF, BLK + BLK // 2, HEAD_DIM)
    for_other = lax.dynamic_index_in_dim(returned, 1 - core, 0, keepdims=False)
    from_other = lax.ppermute(for_other, "core", SWAP)
    so_far = place_call(own_kernel, "place_own", scalars, returned, ())
    return tuple(place_call(other_kernel, "place_other", scalars, from_other, so_far))


def solution(mesh):
    devices = mesh.devices
    fine = Mesh(devices.reshape(4, 4, 2, 8, 2), ("x", "zh", "zl", "y", "core"))
    rows = P(("y", "core", "x", "zh", "zl"), None)
    lists = P(("y", "core"), None)
    return jax.shard_map(
        body,
        mesh=fine,
        in_specs=(rows, rows, rows, rows, lists, lists, lists),
        out_specs=(rows, rows, rows),
        check_vma=False,
    )
```
